256 devices in a mesh: dp: 32 (over x, z), expert: 8 (over y, core).
Axes of the slice: x: 4, y: 4, z: 8, core: 2. Of those that a mesh axis runs over, the one named last changes fastest.
Arguments:
- tokens: bfloat16 [32768, 2048], P(('dp', 'expert')), may hold values from -24 to 24
- expert_ids: int32 [32768, 4], P(('dp', 'expert')), may hold values from 0 to 7, all different within a row; in each aligned block of 128 rows (0 to 127, 128 to 255, ...) at most 128 rows name the same one
- gates: bfloat16 [32768, 4], P(('dp', 'expert')), may hold values from 0.099609375 to 1
- w_gate: bfloat16 [8, 2048, 384], P('expert'), may hold values from -0.125 to 0.125
- w_up: bfloat16 [8, 2048, 384], P('expert'), may hold values from -0.125 to 0.125
- w_down: bfloat16 [8, 384, 2048], P('expert'), may hold values from -0.3125 to 0.3125
- cotangent: bfloat16 [32768, 2048], P(('dp', 'expert')), may hold values from -6 to 6
Outputs:
- mixed: bfloat16 [32768, 2048], P(('dp', 'expert'))
- grad_tokens: bfloat16 [32768, 2048], P(('dp', 'expert'))
- grad_gate: float32 [8, 2048, 384], P('expert', 'dp')
- grad_up: float32 [8, 2048, 384], P('expert', 'dp')
- grad_down: float32 [8, 384, 2048], P('expert', 'dp')
The draws below stay inside these ranges and needn't reach their ends.
Inputs may be any that keep to these rules, and one draw needn't show every extreme that they name: `expert_ids`: each row names 4 different experts. In each aligned block of 128 rows (the rows of one device) no expert is named by more than 128 rows, a bound that some block reaches.
All inputs are finite; a program needn't handle non-finite values.
Results may differ from the reference program's by a relative error of at most 0.024.
Values may be sent and summed in bfloat16 or wider, within the bound.
A program may use at most 128 MiB of HBM per device.

```python
import math
import jax
import jax.numpy as jnp
import numpy as np
from jax import lax

D = 2048
HID = 384
TOPK = 4
TOK_DEV = 128
MOST = 128
EXPERTS = 8
TOKENS = 32768
N_DP = 32
N_EXPERT = 8


def with_spikes(entries, key, source, target, shards_of, factor):
    def block_of(axis_at):
        return (jnp.arange(entries.shape[axis_at]) // (entries.shape[axis_at] // shards_of)).reshape((-1,) + (1,) * (entries.ndim - 1 - axis_at))

    one_side = jax.random.permutation(key, shards_of)[block_of(target)]
    second = (block_of(target) + shards_of // 2) % shards_of
    return jnp.where((block_of(source) == one_side) | (block_of(source) == second), factor * entries, entries)


def level_of(key, dims, split, least, top_value):
    def one(position, parts):
        draws = jax.random.uniform(jax.random.fold_in(jax.random.fold_in(key, 6), position), (parts,), jnp.float32, least / len(split), top_value / len(split))
        return jnp.repeat(jnp.exp(draws), dims[position] // parts).reshape((-1,) + (1,) * (len(dims) - position - 1))

    gain = one(*split[0])
    for cut in split[1:]:
        gain = gain * one(*cut)
    return gain


def shared_out(rng, own, number, rows, amount, top, bound, slope):
    sequence = jax.random.permutation(rng, amount)
    heavy_load, common = shares(amount, rows * top, bound, slope, True), shares(amount, rows * top, bound, slope, False)
    places = jnp.arange(amount)

    def named(sizes, turn):
        used = int((sizes > 0).sum())
        fixed = max(1, used // 4)
        passed = fixed + (places - fixed + turn * (used - fixed)) % max(1, amount - fixed)
        return jnp.zeros((amount,), jnp.int32).at[sequence[jnp.where(places < fixed, places, passed)]].set(jnp.asarray(sizes, jnp.int32))

    sizes = jnp.where(number % 4 == 0, named(heavy_load, number // 4), named(common, number - number // 4 - 1))
    mixed = jax.random.permutation(jax.random.fold_in(own, 3), amount)
    donor, taker = mixed[0:amount // 2 * 2:2], mixed[1:amount // 2 * 2:2]
    margin = jnp.minimum(sizes[donor] - 1, bound - sizes[taker]) // 2
    margin = jnp.where((donor == sequence[0]) | (taker == sequence[0]) | (sizes[taker] == 0), 0, jnp.maximum(margin, 0))
    passed = jax.random.randint(jax.random.fold_in(own, 4), (amount // 2,), 0, 1 << 20) % (margin + 1)
    sizes = sizes.at[donor].add(-passed).at[taker].add(passed)
    members = jnp.searchsorted(jnp.cumsum(sizes), jnp.arange(rows * top), side="right").astype(jnp.int32)
    table = members.reshape(top, rows).T
    table = table[jax.random.permutation(jax.random.fold_in(own, 1), rows)]
    turn = jax.random.randint(jax.random.fold_in(own, 2), (rows, 1), 0, top)
    return jnp.take_along_axis(table, (jnp.arange(top)[None, :] + turn) % top, axis=1)


def shares(count, total, limit, slope, full):
    loads = [(1 << 20) // math.isqrt(standing ** slope) + 1 for standing in range(1, count + 1)]
    largest = limit if full else min(limit, max(-(-total // count), total * loads[0] // sum(loads)))
    least = 1 if total - largest >= count - 1 else 0
    counts, rest = [largest] + [least] * (count - 1), total - largest - least * (count - 1)
    while rest > 0:
        free = [i for i in range(1, count) if counts[i] < largest] or [i for i in range(1, count) if counts[i] < limit]
        pool, left = sum([loads[i] for i in free]), rest
        for i in free:
            more = min(limit - counts[i], max(1, left * loads[i] // pool), rest)
            counts[i] = counts[i] + more
            rest = rest - more
    return np.array(counts)


def bell_draw(stream_key, dims, scale, reach, pieces=(), kind=jnp.bfloat16):
    entries = jax.random.normal(stream_key, dims, jnp.float32) * scale
    if len(pieces) > 0:
        entries = level_of(stream_key, dims, pieces, -0.22, 0.18) * entries
    return jnp.clip(entries, min=-reach, max=reach).astype(kind)


def heavy_noise(key, shape, deviation, most, shards, heavy, held_as=jnp.bfloat16):
    values = deviation * jax.random.normal(key, shape, jnp.float32)
    if shards:
        values = values * level_of(key, shape, shards, -0.22, 0.18)
    return jnp.clip(with_spikes(values, jax.random.fold_in(key, 3), *heavy), -most, most).astype(held_as)


def setup_inputs(seed: int = 0) -> dict:
    key_of = jax.random.split(jax.random.key(seed), 8)
    tokens = heavy_noise(key_of[0], (TOKENS, D), 1.0, 24.0, ((0, 256),), (0, 1, 256, 6.0))
    expert_ids_keys = jax.random.split(jax.random.fold_in(key_of[1], 1), TOKENS // TOK_DEV)
    expert_ids_turns = jax.random.permutation(jax.random.fold_in(key_of[1], 3), TOKENS // TOK_DEV)
    expert_ids = jax.vmap(lambda own, number: shared_out(jax.random.fold_in(key_of[1], 2), own, number, TOK_DEV, EXPERTS, TOPK, MOST, 2))(expert_ids_keys, expert_ids_turns).reshape((TOKENS, TOPK))
    gates = jnp.clip(0.099609375 + 0.9003906 * jax.random.uniform(key_of[2], (TOKENS, TOPK), jnp.float32) ** level_of(key_of[2], (TOKENS, TOPK), ((0, 256),), -0.2, 0.2), 0.099609375, 1.0).astype(jnp.bfloat16)
    w_gate = bell_draw(key_of[3], (EXPERTS, D, HID), D ** -0.5, 0.125, ((0, 8),))
    w_up = bell_draw(key_of[4], (EXPERTS, D, HID), D ** -0.5, 0.125, ((0, 8),))
    w_down = bell_draw(key_of[5], (EXPERTS, HID, D), HID ** -0.5, 0.3125, ((0, 8),))
    cotangent = bell_draw(key_of[6], (TOKENS, D), 1.0, 6.0, ((0, 256),))
    return {"tokens": tokens, "expert_ids": expert_ids, "gates": gates, "w_gate": w_gate, "w_up": w_up, "w_down": w_down, "cotangent": cotangent}


def expert_rows(inputs, out_grads, gate_col, gate_panel, up_panel, down_panel):
    pre_gate = jnp.dot(inputs, gate_panel, preferred_element_type=jnp.float32)
    pre_up = jnp.dot(inputs, up_panel, preferred_element_type=jnp.float32)
    gate_sigmoid = jax.nn.sigmoid(pre_gate)
    activated = (pre_gate * gate_sigmoid * pre_up).astype(jnp.bfloat16)
    expert_out = jnp.dot(activated, down_panel, preferred_element_type=jnp.float32)
    contrib = (gate_col.astype(jnp.float32)[:, None] * expert_out).astype(jnp.bfloat16)
    act_grad = lax.dot_general(out_grads, down_panel, (((1,), (1,)), ((), ())), preferred_element_type=jnp.float32)
    up_grad = (act_grad * pre_gate * gate_sigmoid).astype(jnp.bfloat16)
    pre_grad = (act_grad * pre_up * gate_sigmoid * (1.0 + pre_gate * (1.0 - gate_sigmoid))).astype(jnp.bfloat16)
    grad_rows = lax.dot_general(pre_grad, gate_panel, (((1,), (1,)), ((), ())), preferred_element_type=jnp.float32)
    grad_rows = grad_rows + lax.dot_general(up_grad, up_panel, (((1,), (1,)), ((), ())), preferred_element_type=jnp.float32)
    grad_rows = grad_rows.astype(jnp.bfloat16)
    wgrad_gate = lax.dot_general(inputs, pre_grad, (((0,), (0,)), ((), ())), preferred_element_type=jnp.float32)
    wgrad_up = lax.dot_general(inputs, up_grad, (((0,), (0,)), ((), ())), preferred_element_type=jnp.float32)
    wgrad_down = lax.dot_general(activated, out_grads, (((0,), (0,)), ((), ())), preferred_element_type=jnp.float32)
    return contrib, grad_rows, wgrad_gate, wgrad_up, wgrad_down


def reference(tokens, expert_ids, gates, w_gate, w_up, w_down, cotangent):
    pair_total = TOKENS * TOPK
    room_rows = N_DP * N_EXPERT * MOST
    span_rows = math.gcd(1024, room_rows)
    flat_ids = expert_ids.reshape(pair_total)
    flat_gates = gates.reshape(pair_total)
    pair_index = jnp.arange(pair_total, dtype=jnp.int32)

    def per_expert(state_now, expert_num):
        matches = (flat_ids == expert_num).astype(jnp.int32)
        rank_of = jnp.cumsum(matches) - matches
        target = jnp.where(matches == 1, rank_of, room_rows).astype(jnp.int32)
        chosen = jnp.zeros((room_rows,), jnp.int32).at[target].set(pair_index, mode="drop")
        live_count = jnp.sum(matches).astype(jnp.int32)
        gate_panel = w_gate[expert_num]
        up_panel = w_up[expert_num]
        down_panel = w_down[expert_num]

        def block_step(block_index, inner_state):
            mixed_acc, grad_acc, acc_gate, acc_up, acc_down = inner_state
            start_row = (block_index * span_rows).astype(jnp.int32)
            positions = start_row + jnp.arange(span_rows, dtype=jnp.int32)
            pair_ids = lax.dynamic_slice_in_dim(chosen, start_row, span_rows)
            keep_mask = positions < live_count
            row_index = jnp.where(keep_mask, pair_ids // TOPK, 0).astype(jnp.int32)
            keep_b = keep_mask.astype(jnp.bfloat16)
            inputs = tokens[row_index] * keep_b[:, None]
            gate_col = flat_gates[pair_ids] * keep_b
            out_grads = (gate_col.astype(jnp.float32)[:, None] * cotangent[row_index].astype(jnp.float32)).astype(jnp.bfloat16)
            contrib, grad_rows, wgrad_gate, wgrad_up, wgrad_down = expert_rows(inputs, out_grads, gate_col, gate_panel, up_panel, down_panel)
            dest = jnp.where(keep_mask, row_index, TOKENS).astype(jnp.int32)
            mixed_acc = mixed_acc.at[dest].add(contrib.astype(jnp.float32), mode="drop")
            grad_acc = grad_acc.at[dest].add(grad_rows.astype(jnp.float32), mode="drop")
            return mixed_acc, grad_acc, acc_gate + wgrad_gate, acc_up + wgrad_up, acc_down + wgrad_down

        block_total = (live_count + span_rows - 1) // span_rows
        init = (state_now[0], state_now[1], jnp.zeros((D, HID), jnp.float32), jnp.zeros((D, HID), jnp.float32), jnp.zeros((HID, D), jnp.float32))
        mixed_acc, grad_acc, acc_gate, acc_up, acc_down = lax.fori_loop(0, block_total, block_step, init)
        return (mixed_acc, grad_acc), (acc_gate, acc_up, acc_down)

    start = (jnp.zeros((TOKENS, D), jnp.float32), jnp.zeros((TOKENS, D), jnp.float32))
    (mixed_acc, grad_acc), (grad_gate, grad_up, grad_down) = lax.scan(per_expert, start, jnp.arange(EXPERTS, dtype=jnp.int32))
    return mixed_acc.astype(jnp.bfloat16), grad_acc.astype(jnp.bfloat16), grad_gate, grad_up, grad_down
```

```python
import functools

import jax
import jax.numpy as jnp
from jax import lax
from jax.experimental import pallas as pl
from jax.experimental.pallas import tpu as pltpu
from jax.sharding import PartitionSpec as P

NX, NZ, NY = 4, 8, 4
F32 = jnp.float32
BF16 = jnp.bfloat16
NN = (((1,), (0,)), ((), ()))
NT = (((1,), (1,)), ((), ()))
TN = (((0,), (0,)), ((), ()))
COPIES = 96


def dot(a, b, dims=NN):
    return lax.dot_general(a, b, dims, preferred_element_type=F32)


def add_rows(dst, srcs):
    rows = dst.shape[-2]
    step = 16 if rows % 16 == 0 else rows

    if len(dst.shape) == 2:
        @pl.loop(0, rows // step)
        def _(i):
            sl = pl.ds(pl.multiple_of(i * step, step), step)
            total = dst[sl, :].astype(F32)
            for s in srcs:
                total = total + s[sl, :].astype(F32)
            dst[sl, :] = total.astype(dst.dtype)
    else:
        @pl.loop(0, dst.shape[0])
        def _(i):
            total = dst[i].astype(F32)
            for s in srcs:
                total = total + s[i].astype(F32)
            dst[i] = total.astype(dst.dtype)


def moe_kernel(
    tok, cot, ids_t, gates_t, wg, wu, wd,
    mixed, gtok, ggate, gup, gdown,
    X, C, G, OG, Wgu, Wd, O, SB, RY, PG, APT, PT, Ggu, Gd, RXg, RZgh, RZg, RZdh, RZd, RXd,
    load_sem, send_sem, recv_sem,
):
    T, D = tok.shape
    H = wg.shape[1]
    dp = lax.axis_index("dp")
    ex = lax.axis_index("expert")
    x, z = dp // NZ, dp % NZ
    y, core = ex // 2, ex % 2
    sib = (dp, y * 2 + (1 - core))
    yp = (dp, ((y + 1) % NY) * 2 + core)
    ym = (dp, ((y + NY - 1) % NY) * 2 + core)
    xp = (((x + 1) % NX) * NZ + z, ex)
    xm = (((x + NX - 1) % NX) * NZ + z, ex)
    zp = (x * NZ + (z + 1) % NZ, ex)
    zm = (x * NZ + (z + NZ - 1) % NZ, ex)

    copies = {}

    def reg(name, src, dst, dev):
        copies[name] = (len(copies), src, dst, dev)

    def desc(name):
        k, src, dst, dev = copies[name]
        return pltpu.make_async_remote_copy(
            src_ref=src, dst_ref=dst, send_sem=send_sem.at[k], recv_sem=recv_sem.at[k],
            device_id=dev, device_id_type=pl.DeviceIdType.MESH,
        )

    def start(*names):
        for n in names:
            desc(n).start()

    def recv(*names):
        for n in names:
            desc(n).wait_recv()

    for nm, buf in (("X", X), ("C", C), ("G", G)):
        reg(nm + "s0", buf.at[0, 0], buf.at[0, 1], sib)
        reg(nm + "p", buf.at[0, 0], buf.at[1, 0], yp)
        reg(nm + "m", buf.at[0, 0], buf.at[2, 0], ym)
        for i in (1, 2, 3):
            reg(nm + "s%d" % i, buf.at[i, 0], buf.at[i, 1], sib)
    reg("Xf", X.at[1, 0], X.at[3, 0], yp)
    reg("Gf", G.at[1, 0], G.at[3, 0], yp)
    reg("Cf", C.at[2, 0], C.at[3, 0], ym)
    for i in range(4):
        reg("O%d" % i, O.at[i, 1], SB.at[i], sib)

    def ring4(tag, a, b, r, plus, minus):
        reg(tag + "0", a(2), r(0), plus)
        reg(tag + "1", b(2), r(1), minus)
        reg(tag + "2", b(1), r(2), plus)
        reg(tag + "3", a(-1), r(3), minus)
        reg(tag + "4", a(1), r(4), plus)
        reg(tag + "5", b(-1), r(5), minus)

    def ring4_mid(tag, a, b, r):
        recv(tag + "0")
        add_rows(a(1), [r(0)])
        start(tag + "4")
        recv(tag + "1")
        add_rows(b(-1), [r(1)])
        start(tag + "5")

    slot_of = {0: 0, -1: 1, 1: 2, 2: 3}
    ya = lambda k: O.at[slot_of[k], 0, 0]
    yb = lambda k: O.at[slot_of[k], 0, 1]
    yr = lambda i: RY.at[i]
    ring4("y", ya, yb, yr, yp, ym)

    hz = NZ // 2
    ga = lambda k: Ggu.at[pl.ds(((x + k + NX) % NX) * NZ, hz)]
    gb = lambda k: Ggu.at[pl.ds(((x + k + NX) % NX) * NZ + hz, hz)]
    gr = lambda i: RXg.at[i]
    ring4("gx", ga, gb, gr, xp, xm)

    hd = D // 2
    da = lambda k: Gd.at[z, (x + k + NX) % NX, :, pl.ds(0, hd)]
    db = lambda k: Gd.at[z, (x + k + NX) % NX, :, pl.ds(hd, hd)]
    dr = lambda i: RXd.at[i]
    ring4("dx", da, db, dr, xp, xm)

    def ring8(tag, a, b, full, rh, r, plus, minus):
        reg(tag + "0", a(4), rh(0), plus)
        reg(tag + "1", b(4), rh(1), minus)
        for s, k in ((0, 3), (1, 2), (2, 1)):
            reg(tag + "p%d" % k, full(k), r(2 * s), plus)
            reg(tag + "m%d" % k, full(-k), r(2 * s + 1), minus)

    def ring8_first(tag, a, b, rh):
        recv(tag + "0")
        add_rows(a(3), [rh(0)])
        start(tag + "p3")
        recv(tag + "1")
        add_rows(b(-3), [rh(1)])
        start(tag + "m3")

    def ring8_mid(tag, full, r, k):
        s = 3 - k - 1
        recv(tag + "p%d" % (k + 1))
        add_rows(full(k), [r(2 * s)])
        start(tag + "p%d" % k)
        recv(tag + "m%d" % (k + 1))
        add_rows(full(-k), [r(2 * s + 1)])
        start(tag + "m%d" % k)

    hr = Ggu.shape[1] // 2
    sfull = lambda k: Ggu.at[x * NZ + (z + k + NZ) % NZ]
    sa = lambda k: Ggu.at[x * NZ + (z + k + NZ) % NZ, pl.ds(0, hr)]
    sb = lambda k: Ggu.at[x * NZ + (z + k + NZ) % NZ, pl.ds(hr, hr)]
    srh = lambda i: RZgh.at[i]
    sr = lambda i: RZg.at[i]
    ring8("gz", sa, sb, sfull, srh, sr, zp, zm)

    hx = NX // 2
    efull = lambda k: Gd.at[(z + k + NZ) % NZ]
    ea = lambda k: Gd.at[(z + k + NZ) % NZ, pl.ds(0, hx)]
    eb = lambda k: Gd.at[(z + k + NZ) % NZ, pl.ds(hx, hx)]
    erh = lambda i: RZdh.at[i]
    er = lambda i: RZd.at[i]
    ring8("dz", ea, eb, efull, erh, er, zp, zm)
    assert len(copies) <= COPIES

    loads = [
        pltpu.make_async_copy(tok, X.at[0, 0], load_sem.at[0]),
        pltpu.make_async_copy(cot, C.at[0, 0], load_sem.at[1]),
        pltpu.make_async_copy(wg, Wgu.at[:, pl.ds(0, H)], load_sem.at[2]),
        pltpu.make_async_copy(wu, Wgu.at[:, pl.ds(H, H)], load_sem.at[3]),
        pltpu.make_async_copy(wd, Wd, load_sem.at[4]),
    ]
    for cp in loads:
        cp.start()

    barrier = pltpu.get_barrier_semaphore()
    near = (sib, yp, ym, xp, xm, zp, zm)
    for dev in near:
        pl.semaphore_signal(barrier, inc=1, device_id=dev, device_id_type=pl.DeviceIdType.MESH)

    rows16 = lax.broadcasted_iota(jnp.int32, (16, T), 0)
    dense = jnp.zeros((16, T), F32)
    for k in range(ids_t.shape[0]):
        dense = dense + jnp.where(ids_t[k : k + 1, :] == rows16, gates_t[k : k + 1, :].astype(F32), 0.0)
    G[0, 0] = dense.astype(BF16)

    per = H // (NX * NZ)
    q = lax.broadcasted_iota(jnp.int32, PT.shape, 0)
    unit = lax.broadcasted_iota(jnp.int32, PT.shape, 1)
    j = q & 15
    wanted = (((q >> 4) & (NX - 1)) * NZ + (q >> 6)) * per + j
    PT[...] = jnp.where((unit == wanted) & (j < per), 1.0, 0.0).astype(BF16)

    pl.semaphore_wait(barrier, len(near))
    loads[0].wait()
    loads[1].wait()
    start("Xp", "Cm", "Gp", "Gm", "Gs0", "Xs0", "Cs0", "Cp", "Xm")
    for cp in loads[2:]:
        cp.wait()

    mine = (rows16 == ex).astype(F32).astype(BF16)

    def compute(i):
        gate = jnp.concatenate([dot(G[i, s], mine, TN)[:, :1] for s in (0, 1)], axis=0)
        rows = pl.ds(pl.multiple_of(i * 2 * T, 2 * T), 2 * T)
        inputs = X[i].reshape(2 * T, D)
        out_grad = (C[i].reshape(2 * T, D).astype(F32) * gate).astype(BF16)
        OG[rows, :] = out_grad
        pre = dot(inputs, Wgu[...])
        act_grad = dot(out_grad, Wd[...], NT)
        pre_gate, pre_up = pre[:, :H], pre[:, H:]
        sig = 1.0 / (1.0 + jnp.exp(-pre_gate))
        silu = pre_gate * sig
        activated = (silu * pre_up).astype(BF16)
        PG[rows, H:] = (act_grad * silu).astype(BF16)
        PG[rows, :H] = (act_grad * pre_up * sig * (1.0 + pre_gate * (1.0 - sig))).astype(BF16)
        APT[:, rows] = dot(PT[...], activated, NT).astype(BF16)

        @pl.loop(0, D // 512)
        def _(n):
            cols = pl.ds(pl.multiple_of(n * 512, 512), 512)
            part = (dot(activated, Wd[:, cols]) * gate).astype(BF16)
            grad = dot(PG[rows, :], Wgu[cols, :], NT).astype(BF16)
            for s in (0, 1):
                O[i, s, 0, :, cols] = part[s * T : (s + 1) * T]
                O[i, s, 1, :, cols] = grad[s * T : (s + 1) * T]

    def fold(i):
        recv("O%d" % i)
        for a in (0, 1):
            add_rows(O.at[i, 0, a], [SB.at[i, a]])

    def step(i, carry):
        @pl.when(i == 0)
        def _():
            recv("Xs0", "Cs0", "Gs0")

        @pl.when(i == 1)
        def _():
            recv("Xp", "Cm", "Gp", "Gm")
            start("Xf", "Cf", "Gf", "Gs1", "Gs2", "Xs1", "Cs2")
            recv("Cp", "Xm")
            start("Cs1", "Xs2")
            recv("Xs1", "Cs1", "Gs1")

        @pl.when(i == 2)
        def _():
            recv("Xs2", "Cs2", "Gs2")

        @pl.when(i == 3)
        def _():
            recv("Xf", "Cf", "Gf")
            start("Gs3", "Xs3", "Cs3")
            fold(1)
            start("y3")
            recv("Xs3", "Cs3", "Gs3")

        compute(i)
        for k in range(4):
            @pl.when(i == k)
            def _():
                start("O%d" % k)
        return carry

    lax.fori_loop(0, 4, step, 0)

    dims3 = (4, Ggu.shape[1], 2 * H)

    @pl.loop(0, D // 256)
    def _(m):
        cols = pl.ds(pl.multiple_of(m * 256, 256), 256)
        Ggu[pl.ds(m * 4, 4)] = (
            dot(X[:, :, :, cols].reshape(8 * T, 256), PG[...], TN).astype(BF16).reshape(dims3)
        )

    start("gx0", "gx1", "gx2", "gx3")
    fold(3)
    start("y0", "y1")
    fold(2)
    start("y2")

    @pl.loop(0, D // 512)
    def _(n):
        cols = pl.ds(pl.multiple_of(n * 512, 512), 512)
        Gd[:, :, :, cols] = dot(APT[...], OG[:, cols]).astype(BF16).reshape(NZ, NX, 16, 512)

    start("dz0", "dz1")
    fold(0)
    ring8_first("dz", ea, eb, erh)
    ring4_mid("gx", ga, gb, gr)
    ring8_mid("dz", efull, er, 2)
    ring4_mid("y", ya, yb, yr)
    ring8_mid("dz", efull, er, 1)
    recv("dzp1", "dzm1")
    add_rows(efull(0), [er(4), er(5)])
    start("dx0", "dx1", "dx2", "dx3")
    recv("gx3", "gx4")
    add_rows(ga(0), [gr(3), gr(4)])
    recv("gx2", "gx5")
    add_rows(gb(0), [gr(2), gr(5)])
    start("gz0", "gz1")
    ring4_mid("dx", da, db, dr)
    ring8_first("gz", sa, sb, srh)
    recv("y2", "y3", "y4", "y5")

    @pl.loop(0, T // 16)
    def _(i):
        sl = pl.ds(pl.multiple_of(i * 16, 16), 16)
        mixed[sl, :] = (
            O[0, 0, 0, sl, :].astype(F32) + RY[3, sl, :].astype(F32) + RY[4, sl, :].astype(F32)
        ).astype(BF16)
        gtok[sl, :] = (
            O[0, 0, 1, sl, :].astype(F32) + RY[2, sl, :].astype(F32) + RY[5, sl, :].astype(F32)
        ).astype(BF16)

    ring8_mid("gz", sfull, sr, 2)
    recv("dx2", "dx3", "dx4", "dx5")
    low = da(0)[...].astype(F32) + RXd[3].astype(F32) + RXd[4].astype(F32)
    high = db(0)[...].astype(F32) + RXd[2].astype(F32) + RXd[5].astype(F32)
    gdown[:, :hd] = low[:per]
    gdown[:, hd:] = high[:per]
    ring8_mid("gz", sfull, sr, 1)
    recv("gzp1", "gzm1")
    total = sfull(0)[...].astype(F32) + RZg[4].astype(F32) + RZg[5].astype(F32)
    ggate[...] = total[:, :H]
    gup[...] = total[:, H:]

    for n in copies:
        desc(n).wait_send()


def per_device(tokens, expert_ids, gates, w_gate, w_up, w_down, cotangent):
    T, D = tokens.shape
    H = w_gate.shape[2]
    rows = D // (NX * NZ)
    per = H // (NX * NZ)
    hbm = pl.BlockSpec(memory_space=pl.ANY)
    vmem = pl.BlockSpec(memory_space=pltpu.VMEM)
    V = pltpu.VMEM
    flops = 2 * 8 * T * D * H * 9
    mixed, gtok, ggate, gup, gdown = pl.pallas_call(
        moe_kernel,
        out_shape=(
            jax.ShapeDtypeStruct((T, D), BF16),
            jax.ShapeDtypeStruct((T, D), BF16),
            jax.ShapeDtypeStruct((rows, H), F32),
            jax.ShapeDtypeStruct((rows, H), F32),
            jax.ShapeDtypeStruct((per, D), F32),
        ),
        in_specs=[hbm, hbm, vmem, vmem, hbm, hbm, hbm],
        out_specs=(vmem,) * 5,
        scratch_shapes=[
            V((4, 2, T, D), BF16),
            V((4, 2, T, D), BF16),
            V((4, 2, 16, T), BF16),
            V((8 * T, D), BF16),
            V((D, 2 * H), BF16),
            V((H, D), BF16),
            V((4, 2, 2, T, D), BF16),
            V((4, 2, T, D), BF16),
            V((6, T, D), BF16),
            V((8 * T, 2 * H), BF16),
            V((NX * NZ * 16, 8 * T), BF16),
            V((NX * NZ * 16, H), BF16),
            V((NX * NZ, rows, 2 * H), BF16),
            V((NZ, NX, 16, D), BF16),
            V((6, NZ // 2, rows, 2 * H), BF16),
            V((2, rows // 2, 2 * H), BF16),
            V((6, rows, 2 * H), BF16),
            V((2, NX // 2, 16, D), BF16),
            V((6, NX, 16, D), BF16),
            V((6, 16, D // 2), BF16),
            pltpu.SemaphoreType.DMA((5,)),
            pltpu.SemaphoreType.DMA((COPIES,)),
            pltpu.SemaphoreType.DMA((COPIES,)),
        ],
        compiler_params=pltpu.CompilerParams(
            collective_id=0, has_side_effects=True, vmem_limit_bytes=60 * 2**20
        ),
        cost_estimate=pl.CostEstimate(flops=flops, bytes_accessed=32 << 20, transcendentals=8 * T * H),
        name="moe",
    )(tokens, cotangent, expert_ids.T, gates.T, w_gate[0], w_up[0], w_down[0])
    return mixed, gtok, ggate[None], gup[None], gdown[None]


def solution(mesh):
    return jax.shard_map(
        per_device,
        mesh=mesh,
        in_specs=(
            P(("dp", "expert"), None),
            P(("dp", "expert"), None),
            P(("dp", "expert"), None),
            P("expert", None, None),
            P("expert", None, None),
            P("expert", None, None),
            P(("dp", "expert"), None),
        ),
        out_specs=(
            P(("dp", "expert"), None),
            P(("dp", "expert"), None),
            P("expert", "dp", None),
            P("expert", "dp", None),
            P("expert", "dp", None),
        ),
        check_vma=False,
    )
```

```python
import functools

import jax
import jax.numpy as jnp
from jax import lax
from jax.experimental import pallas as pl
from jax.experimental.pallas import tpu as pltpu
from jax.sharding import PartitionSpec as P

NX, NZ, NY = 4, 8, 4
F32 = jnp.float32
BF16 = jnp.bfloat16
NN = (((1,), (0,)), ((), ()))
NT = (((1,), (1,)), ((), ()))
TN = (((0,), (0,)), ((), ()))
COPIES = 96


def dot(a, b, dims=NN):
    return lax.dot_general(a, b, dims, preferred_element_type=F32)


def add_rows(dst, srcs):
    rows = dst.shape[-2]
    step = 16 if rows % 16 == 0 else rows

    if len(dst.shape) == 2:
        @pl.loop(0, rows // step)
        def _(i):
            sl = pl.ds(pl.multiple_of(i * step, step), step)
            total = dst[sl, :].astype(F32)
            for s in srcs:
                total = total + s[sl, :].astype(F32)
            dst[sl, :] = total.astype(dst.dtype)
    else:
        @pl.loop(0, dst.shape[0])
        def _(i):
            total = dst[i].astype(F32)
            for s in srcs:
                total = total + s[i].astype(F32)
            dst[i] = total.astype(dst.dtype)


def moe_kernel(
    tok, cot, ids_t, gates_t, wg, wu, wd,
    mixed, gtok, ggate, gup, gdown,
    X, C, G, OG, Wgu, Wd, O, SB, RY, PG, ACT, GC, APT, PT, GACC, DACC,
    S1, S2, S3, S3x, R1, R1h, R1z, R2h, R2z, R2x, R3h, R3z, R3x,
    load_sem, send_sem, recv_sem,
):
    T, D = tok.shape
    H = wg.shape[1]
    CX = S1.shape[3]
    per = H // (NX * NZ)
    dp = lax.axis_index("dp")
    ex = lax.axis_index("expert")
    x, z = dp // NZ, dp % NZ
    y, core = ex // 2, ex % 2
    sib = (dp, y * 2 + (1 - core))
    yp = (dp, ((y + 1) % NY) * 2 + core)
    ym = (dp, ((y + NY - 1) % NY) * 2 + core)
    xp = (((x + 1) % NX) * NZ + z, ex)
    xm = (((x + NX - 1) % NX) * NZ + z, ex)
    zp = (x * NZ + (z + 1) % NZ, ex)
    zm = (x * NZ + (z + NZ - 1) % NZ, ex)
    at_x = lambda k: (x + k + NX) % NX
    at_z = lambda k: (z + k + NZ) % NZ

    copies = {}

    def reg(name, src, dst, dev):
        copies[name] = (len(copies), src, dst, dev)

    def desc(name):
        k, src, dst, dev = copies[name]
        return pltpu.make_async_remote_copy(
            src_ref=src, dst_ref=dst, send_sem=send_sem.at[k], recv_sem=recv_sem.at[k],
            device_id=dev, device_id_type=pl.DeviceIdType.MESH,
        )

    def start(*names):
        for n in names:
            desc(n).start()

    def recv(*names):
        for n in names:
            desc(n).wait_recv()

    for nm, buf in (("X", X), ("C", C), ("G", G)):
        reg(nm + "s0", buf.at[0, 0], buf.at[0, 1], sib)
        reg(nm + "p", buf.at[0, 0], buf.at[1, 0], yp)
        reg(nm + "m", buf.at[0, 0], buf.at[2, 0], ym)
        for i in (1, 2, 3):
            reg(nm + "s%d" % i, buf.at[i, 0], buf.at[i, 1], sib)
    reg("Xf", X.at[1, 0], X.at[3, 0], yp)
    reg("Gf", G.at[1, 0], G.at[3, 0], yp)
    reg("Cf", C.at[2, 0], C.at[3, 0], ym)
    for i in range(4):
        reg("O%d" % i, O.at[i, 1], SB.at[i], sib)

    def ring4(tag, a, b, r, plus, minus):
        reg(tag + "0", a(2), r(0), plus)
        reg(tag + "1", b(2), r(1), minus)
        reg(tag + "2", b(1), r(2), plus)
        reg(tag + "3", a(-1), r(3), minus)
        reg(tag + "4", a(1), r(4), plus)
        reg(tag + "5", b(-1), r(5), minus)

        def mid():
            recv(tag + "0")
            add_rows(a(1), [r(0)])
            start(tag + "4")
            recv(tag + "1")
            add_rows(b(-1), [r(1)])
            start(tag + "5")

        return mid

    def ring8(tag, a, b, full, rh, r, plus, minus):
        reg(tag + "0", a(4), rh(0), plus)
        reg(tag + "1", b(4), rh(1), minus)
        for s, k in ((0, 3), (1, 2), (2, 1)):
            reg(tag + "p%d" % k, full(k), r(2 * s), plus)
            reg(tag + "m%d" % k, full(-k), r(2 * s + 1), minus)

        def hop(k):
            if k == 3:
                recv(tag + "0")
                add_rows(a(3), [rh(0)])
                start(tag + "p3")
                recv(tag + "1")
                add_rows(b(-3), [rh(1)])
                start(tag + "m3")
                return
            s = 2 - k
            recv(tag + "p%d" % (k + 1))
            add_rows(full(k), [r(2 * s)])
            start(tag + "p%d" % k)
            recv(tag + "m%d" % (k + 1))
            add_rows(full(-k), [r(2 * s + 1)])
            start(tag + "m%d" % k)

        return hop

    slot_of = {0: 0, -1: 1, 1: 2, 2: 3}
    HT = T // 2
    y_mid = []
    for p in (0, 1):
        piece = pl.ds(p * HT, HT)
        y_mid.append(ring4(
            "y%d" % p,
            lambda k, piece=piece: O.at[slot_of[k], 0, 0, piece],
            lambda k, piece=piece: O.at[slot_of[k], 0, 1, piece],
            lambda i, piece=piece: RY.at[i, piece],
            yp, ym,
        ))

    hz = NZ // 2
    a1 = lambda k: S1.at[at_x(k), pl.ds(0, hz)]
    b1 = lambda k: S1.at[at_x(k), pl.ds(hz, hz)]
    r1 = lambda i: R1.at[i]
    s1_mid = ring4("s1x", a1, b1, r1, xp, xm)
    rows = S1.shape[2]
    hr = rows // 2
    f1z = lambda k: S1.at[x, at_z(k)]
    s1_hop = ring8(
        "s1z",
        lambda k: S1.at[x, at_z(k), pl.ds(0, hr)],
        lambda k: S1.at[x, at_z(k), pl.ds(hr, hr)],
        f1z, lambda i: R1h.at[i], lambda i: R1z.at[i], zp, zm,
    )

    hx = NX // 2
    f2 = lambda k: S2.at[at_z(k)]
    s2_hop = ring8(
        "s2z",
        lambda k: S2.at[at_z(k), pl.ds(0, hx)],
        lambda k: S2.at[at_z(k), pl.ds(hx, hx)],
        f2, lambda i: R2h.at[i], lambda i: R2z.at[i], zp, zm,
    )
    a2 = lambda k: S2.at[z, at_x(k), pl.ds(0, hr)]
    b2 = lambda k: S2.at[z, at_x(k), pl.ds(hr, hr)]
    s2_mid = ring4("s2x", a2, b2, lambda i: R2x.at[i], xp, xm)

    hd = D // 2
    f3 = lambda k: S3.at[at_z(k)]
    s3_hop = ring8(
        "s3z",
        lambda k: S3.at[at_z(k), :, pl.ds(0, hd)],
        lambda k: S3.at[at_z(k), :, pl.ds(hd, hd)],
        f3, lambda i: R3h.at[i], lambda i: R3z.at[i], zp, zm,
    )
    a3 = lambda k: S3x.at[at_x(k), :, pl.ds(0, hd)]
    b3 = lambda k: S3x.at[at_x(k), :, pl.ds(hd, hd)]
    s3_mid = ring4("s3x", a3, b3, lambda i: R3x.at[i], xp, xm)
    assert len(copies) <= COPIES

    loads = [
        pltpu.make_async_copy(tok, X.at[0, 0], load_sem.at[0]),
        pltpu.make_async_copy(cot, C.at[0, 0], load_sem.at[1]),
        pltpu.make_async_copy(wg, Wgu.at[:, pl.ds(0, H)], load_sem.at[2]),
        pltpu.make_async_copy(wu, Wgu.at[:, pl.ds(H, H)], load_sem.at[3]),
        pltpu.make_async_copy(wd, Wd, load_sem.at[4]),
    ]
    for cp in loads:
        cp.start()

    barrier = pltpu.get_barrier_semaphore()
    near = (sib, yp, ym, xp, xm, zp, zm)
    for dev in near:
        pl.semaphore_signal(barrier, inc=1, device_id=dev, device_id_type=pl.DeviceIdType.MESH)

    rows16 = lax.broadcasted_iota(jnp.int32, (16, T), 0)
    dense = jnp.zeros((16, T), F32)
    for k in range(ids_t.shape[0]):
        dense = dense + jnp.where(ids_t[k : k + 1, :] == rows16, gates_t[k : k + 1, :].astype(F32), 0.0)
    G[0, 0] = dense.astype(BF16)

    loads[0].wait()
    loads[1].wait()
    pl.semaphore_wait(barrier, len(near))
    start("Xp", "Cm", "Gp", "Gm", "Gs0", "Xs0", "Cs0", "Cp", "Xm")

    q = lax.broadcasted_iota(jnp.int32, PT.shape, 0)
    unit = lax.broadcasted_iota(jnp.int32, PT.shape, 1)
    row = ((unit // per) % NZ) * (NX * per) + (unit // (per * NZ)) * per + unit % per
    PT[...] = jnp.where(q == row, 1.0, 0.0).astype(BF16)

    for cp in loads[2:]:
        cp.wait()

    mine = (rows16 == ex).astype(F32).astype(BF16)

    def rows_of(i):
        return pl.ds(pl.multiple_of(i * 2 * T, 2 * T), 2 * T)

    def hidden(i):
        gate = jnp.concatenate([dot(G[i, s], mine, TN) for s in (0, 1)], axis=0)
        GC[...] = gate
        gate = gate[:, :1]
        here = rows_of(i)
        inputs = X[i].reshape(2 * T, D)
        out_grad = (C[i].reshape(2 * T, D).astype(F32) * gate).astype(BF16)
        OG[here, :] = out_grad
        pre = dot(inputs, Wgu[...])
        act_grad = dot(out_grad, Wd[...], NT)
        pre_gate, pre_up = pre[:, :H], pre[:, H:]
        sig = 1.0 / (1.0 + jnp.exp(-pre_gate))
        silu = pre_gate * sig
        activated = (silu * pre_up).astype(BF16)
        ACT[...] = activated
        PG[here, H:] = (act_grad * silu).astype(BF16)
        PG[here, :H] = (act_grad * pre_up * sig * (1.0 + pre_gate * (1.0 - sig))).astype(BF16)
        APT[:, here] = dot(PT[...], activated, NT).astype(BF16)

    def outputs(i):
        @pl.loop(0, D // 512)
        def _(n):
            cols = pl.ds(pl.multiple_of(n * 512, 512), 512)
            part = (dot(ACT[...], Wd[:, cols]) * GC[:, :1]).astype(BF16)
            grad = dot(PG[rows_of(i), :], Wgu[cols, :], NT).astype(BF16)
            for s in (0, 1):
                O[i, s, 0, :, cols] = part[s * T : (s + 1) * T]
                O[i, s, 1, :, cols] = grad[s * T : (s + 1) * T]

    def gate_up_part(m, first, count):
        cols = pl.ds(pl.multiple_of(m * 256, 256), 256)
        span = pl.ds(first * 2 * T, count * 2 * T)
        return dot(X[pl.ds(first, count), :, :, cols].reshape(count * 2 * T, 256), PG[span, :], TN)

    def down_part(n, first, count):
        cols = pl.ds(pl.multiple_of(n * 512, 512), 512)
        span = pl.ds(first * 2 * T, count * 2 * T)
        return dot(APT[:, span], OG[span, cols])

    def partial(first, count, fresh):
        @pl.loop(0, D // 256)
        def _(m):
            here = pl.ds(pl.multiple_of(m * 256, 256), 256)
            new = gate_up_part(m, first, count)
            GACC[here, :] = new if fresh else GACC[here, :] + new

        @pl.loop(0, D // 512)
        def _(n):
            cols = pl.ds(pl.multiple_of(n * 512, 512), 512)
            new = down_part(n, first, count)
            DACC[:, cols] = new if fresh else DACC[:, cols] + new

    def finish():
        @pl.loop(0, D // 512)
        def _(n):
            cols = pl.ds(pl.multiple_of(n * 512, 512), 512)
            S3[:, :, cols] = (DACC[:, cols] + down_part(n, 3, 1)).astype(BF16).reshape(NZ, NX * per, 512)

        start("s3z0", "s3z1")

        @pl.loop(0, 8)
        def _(t):
            k = t // 2
            xx = (x + jnp.where(k == 0, 2, jnp.where(k == 1, 1, jnp.where(k == 2, 3, 0)))) % NX
            half = t % 2
            m = xx * 2 + half
            here = pl.ds(pl.multiple_of(m * 256, 256), 256)
            new = (GACC[here, :] + gate_up_part(m, 3, 1)).astype(BF16)
            S1[xx, pl.ds(half * hz, hz)] = new[:, :CX].reshape(hz, rows, CX)
            S2[pl.ds(half * hz, hz), xx] = new[:, CX:].reshape(hz, rows, 2 * H - CX)
            for at, name in ((0, "s1x0"), (1, "s1x1"), (3, "s1x2"), (4, "s1x3")):
                @pl.when(t == at)
                def _():
                    start(name)

        start("s2z0", "s2z1")

    def fold(i):
        recv("O%d" % i)
        for a in (0, 1):
            add_rows(O.at[i, 0, a], [SB.at[i, a]])

    def step(i, carry):
        @pl.when(i == 0)
        def _():
            recv("Xs0", "Cs0", "Gs0")

        @pl.when(i == 1)
        def _():
            partial(0, 1, True)
            recv("Xp", "Cm", "Gp", "Gm")
            start("Xf", "Cf", "Gf", "Gs1", "Gs2", "Xs1", "Cs2")
            recv("Cp", "Xm")
            start("Cs1", "Xs2")
            recv("Xs1", "Cs1", "Gs1")

        @pl.when(i == 2)
        def _():
            recv("Xs2", "Cs2", "Gs2")

        @pl.when(i == 3)
        def _():
            fold(1)
            start("y03", "y13")
            fold(2)
            start("y02", "y12")
            recv("Xf", "Cf", "Gf")
            start("Gs3", "Xs3", "Cs3")
            partial(1, 2, False)
            recv("Xs3", "Cs3", "Gs3")

        hidden(i)

        @pl.when(i == 3)
        def _():
            finish()

        outputs(i)
        for k in range(4):
            @pl.when(i == k)
            def _():
                start("O%d" % k)
        return carry

    lax.fori_loop(0, 4, step, 0)

    def y_final(p):
        recv("y%d2" % p, "y%d3" % p, "y%d4" % p, "y%d5" % p)

        @pl.loop(0, HT // 16)
        def _(i):
            sl = pl.ds(pl.multiple_of(p * HT + i * 16, 16), 16)
            mixed[sl, :] = (
                O[0, 0, 0, sl, :].astype(F32) + RY[3, sl, :].astype(F32) + RY[4, sl, :].astype(F32)
            ).astype(BF16)
            gtok[sl, :] = (
                O[0, 0, 1, sl, :].astype(F32) + RY[2, sl, :].astype(F32) + RY[5, sl, :].astype(F32)
            ).astype(BF16)

    s3_hop(3)
    fold(3)
    start("y00", "y01", "y10", "y11")
    s2_hop(3)
    s1_mid()
    fold(0)
    s3_hop(2)
    s2_hop(2)
    y_mid[0]()
    s3_hop(1)
    recv("s1x3", "s1x4")
    add_rows(a1(0), [r1(3), r1(4)])
    recv("s1x2", "s1x5")
    add_rows(b1(0), [r1(2), r1(5)])
    start("s1z0", "s1z1")
    y_mid[1]()
    s2_hop(1)
    s1_hop(3)

    recv("s3zp1", "s3zm1")
    p_row = lax.broadcasted_iota(jnp.int32, (NX * 16, NX * per), 0)
    p_unit = lax.broadcasted_iota(jnp.int32, (NX * 16, NX * per), 1)
    apart = jnp.where(p_row == (p_unit // per) * 16 + p_unit % per, 1.0, 0.0).astype(BF16)

    @pl.loop(0, D // 512)
    def _(n):
        cols = pl.ds(pl.multiple_of(n * 512, 512), 512)
        total = S3[z, :, cols].astype(F32) + R3z[4, :, cols].astype(F32) + R3z[5, :, cols].astype(F32)
        S3x[:, :, cols] = dot(apart, total.astype(BF16)).astype(BF16).reshape(NX, 16, 512)

    start("s3x0", "s3x1", "s3x2", "s3x3")
    s1_hop(2)
    recv("s2zp1", "s2zm1")
    add_rows(f2(0), [R2z.at[4], R2z.at[5]])
    start("s2x0", "s2x1", "s2x2", "s2x3")
    s3_mid()
    y_final(0)
    s1_hop(1)
    s2_mid()
    recv("s3x2", "s3x3", "s3x4", "s3x5")
    low = a3(0)[...].astype(F32) + R3x[3].astype(F32) + R3x[4].astype(F32)
    high = b3(0)[...].astype(F32) + R3x[2].astype(F32) + R3x[5].astype(F32)
    for j in range(per):
        gdown[j, :, :hd] = low[j : j + 1]
        gdown[j, :, hd:] = high[j : j + 1]
    y_final(1)
    recv("s2x2", "s2x3", "s2x4", "s2x5")
    gup[:hr, CX - H :] = a2(0)[...].astype(F32) + R2x[3].astype(F32) + R2x[4].astype(F32)
    gup[hr:, CX - H :] = b2(0)[...].astype(F32) + R2x[2].astype(F32) + R2x[5].astype(F32)
    recv("s1zp1", "s1zm1")
    total = f1z(0)[...].astype(F32) + R1z[4].astype(F32) + R1z[5].astype(F32)
    ggate[...] = total[:, :H]
    gup[:, : CX - H] = total[:, H:]

    for n in copies:
        desc(n).wait_send()


def copy_kernel(*refs):
    half = len(refs) // 2
    for k in range(half):
        refs[half + k][...] = refs[k][...]


def per_device(tokens, expert_ids, gates, w_gate, w_up, w_down, cotangent):
    T, D = tokens.shape
    H = w_gate.shape[2]
    rows = D // (NX * NZ)
    per = H // (NX * NZ)
    hbm = pl.BlockSpec(memory_space=pl.ANY)
    vmem = pl.BlockSpec(memory_space=pltpu.VMEM)
    V = pltpu.VMEM
    CX = 512
    CZ = 2 * H - CX
    flops = 2 * 8 * T * D * H * 9
    shapes = (
        jax.ShapeDtypeStruct((T, D), BF16),
        jax.ShapeDtypeStruct((T, D), BF16),
        jax.ShapeDtypeStruct((rows, H), F32),
        jax.ShapeDtypeStruct((rows, H), F32),
        jax.ShapeDtypeStruct((per, 1, D), F32),
    )
    outs = pl.pallas_call(
        moe_kernel,
        out_shape=shapes,
        in_specs=[hbm, hbm, vmem, vmem, hbm, hbm, hbm],
        out_specs=(vmem,) * 5,
        scratch_shapes=[
            V((4, 2, T, D), BF16),
            V((4, 2, T, D), BF16),
            V((4, 2, 16, T), BF16),
            V((8 * T, D), BF16),
            V((D, 2 * H), BF16),
            V((H, D), BF16),
            V((4, 2, 2, T, D), BF16),
            V((4, 2, T, D), BF16),
            V((6, T, D), BF16),
            V((8 * T, 2 * H), BF16),
            V((2 * T, H), BF16),
            V((2 * T, 128), F32),
            V((H, 8 * T), BF16),
            V((H, H), BF16),
            V((D, 2 * H), F32),
            V((H, D), F32),
            V((NX, NZ, rows, CX), BF16),
            V((NZ, NX, rows, CZ), BF16),
            V((NZ, NX * per, D), BF16),
            V((NX, 16, D), BF16),
            V((6, NZ // 2, rows, CX), BF16),
            V((2, rows // 2, CX), BF16),
            V((6, rows, CX), BF16),
            V((2, NX // 2, rows, CZ), BF16),
            V((6, NX, rows, CZ), BF16),
            V((6, rows // 2, CZ), BF16),
            V((2, NX * per, D // 2), BF16),
            V((6, NX * per, D), BF16),
            V((6, 16, D // 2), BF16),
            pltpu.SemaphoreType.DMA((5,)),
            pltpu.SemaphoreType.DMA((COPIES,)),
            pltpu.SemaphoreType.DMA((COPIES,)),
        ],
        compiler_params=pltpu.CompilerParams(
            collective_id=0, has_side_effects=True, vmem_limit_bytes=63 * 2**20
        ),
        cost_estimate=pl.CostEstimate(flops=flops, bytes_accessed=32 << 20, transcendentals=8 * T * H),
        name="moe",
    )(tokens, cotangent, expert_ids.T, gates.T, w_gate[0], w_up[0], w_down[0])
    mixed, gtok, ggate, gup, gdown = pl.pallas_call(
        copy_kernel,
        out_shape=shapes,
        in_specs=[vmem] * 5,
        out_specs=(vmem,) * 5,
        name="hand_out",
    )(*outs)
    return mixed, gtok, ggate[None], gup[None], gdown.reshape(1, per, D)


def solution(mesh):
    return jax.shard_map(
        per_device,
        mesh=mesh,
        in_specs=(
            P(("dp", "expert"), None),
            P(("dp", "expert"), None),
            P(("dp", "expert"), None),
            P("expert", None, None),
            P("expert", None, None),
            P("expert", None, None),
            P(("dp", "expert"), None),
        ),
        out_specs=(
            P(("dp", "expert"), None),
            P(("dp", "expert"), None),
            P("expert", "dp", None),
            P("expert", "dp", None),
            P("expert", "dp", None),
        ),
        check_vma=False,
    )
```

```python
import functools

import jax
import jax.numpy as jnp
from jax import lax
from jax.experimental import pallas as pl
from jax.experimental.pallas import tpu as pltpu
from jax.sharding import PartitionSpec as P

NX, NZ, NY = 4, 8, 4
F32 = jnp.float32
BF16 = jnp.bfloat16
NN = (((1,), (0,)), ((), ()))
NT = (((1,), (1,)), ((), ()))
TN = (((0,), (0,)), ((), ()))
COPIES = 112


def dot(a, b, dims=NN):
    return lax.dot_general(a, b, dims, preferred_element_type=F32)


def add_rows(dst, srcs):
    rows = dst.shape[-2]
    step = 16 if rows % 16 == 0 else rows

    if len(dst.shape) == 2:
        @pl.loop(0, rows // step)
        def _(i):
            sl = pl.ds(pl.multiple_of(i * step, step), step)
            total = dst[sl, :].astype(F32)
            for s in srcs:
                total = total + s[sl, :].astype(F32)
            dst[sl, :] = total.astype(dst.dtype)
    else:
        @pl.loop(0, dst.shape[0])
        def _(i):
            total = dst[i].astype(F32)
            for s in srcs:
                total = total + s[i].astype(F32)
            dst[i] = total.astype(dst.dtype)


def moe_kernel(
    tok, cot, ids_t, gates_t, wg, wu, wd,
    mixed, gtok, ggate, gup, gdown,
    X, C, G, GT, OG, Wgu, Wd, O, SB, RY, PG, ACT, GC, APT, PT, GACC, DACC,
    S1, S2, S3, S3x, R1, R1h, R1z, R2h, R2z, R2x, R3h, R3z, R3x,
    load_sem, send_sem, recv_sem,
):
    T, D = tok.shape
    H = wg.shape[1]
    CX = 2 * S1.shape[4]
    per = H // (NX * NZ)
    dp = lax.axis_index("dp")
    ex = lax.axis_index("expert")
    x, z = dp // NZ, dp % NZ
    y, core = ex // 2, ex % 2
    sib = (dp, y * 2 + (1 - core))
    yp = (dp, ((y + 1) % NY) * 2 + core)
    ym = (dp, ((y + NY - 1) % NY) * 2 + core)
    xp = (((x + 1) % NX) * NZ + z, ex)
    xm = (((x + NX - 1) % NX) * NZ + z, ex)
    zp = (x * NZ + (z + 1) % NZ, ex)
    zm = (x * NZ + (z + NZ - 1) % NZ, ex)
    at_x = lambda k: (x + k + NX) % NX
    at_z = lambda k: (z + k + NZ) % NZ

    copies = {}

    def reg(name, src, dst, dev):
        copies[name] = (len(copies), src, dst, dev)

    def desc(name):
        k, src, dst, dev = copies[name]
        return pltpu.make_async_remote_copy(
            src_ref=src, dst_ref=dst, send_sem=send_sem.at[k], recv_sem=recv_sem.at[k],
            device_id=dev, device_id_type=pl.DeviceIdType.MESH,
        )

    def start(*names):
        for n in names:
            desc(n).start()

    def recv(*names):
        for n in names:
            desc(n).wait_recv()

    HT = T // 2
    for nm, buf in (("X", X), ("C", C)):
        for i in range(4):
            reg(nm + "s%d" % i, buf.at[i, :, 0], buf.at[i, :, 1], sib)
        for h in (0, 1):
            reg(nm + "p%d" % h, buf.at[0, h, 0], buf.at[1 + h, 0, 0], yp)
            reg(nm + "m%d" % h, buf.at[0, h, 0], buf.at[1 + h, 1, 0], ym)
        reg(nm + "f0", buf.at[1, 0, 0], buf.at[3, 0, 0], yp)
        reg(nm + "f1", buf.at[2, 1, 0], buf.at[3, 1, 0], ym)
    for i in range(4):
        reg("Gs%d" % i, G.at[i, 0], G.at[i, 1], sib)
    reg("Gp", G.at[0, 0], G.at[1, 0], yp)
    reg("Gm", G.at[0, 0], G.at[2, 0], ym)
    reg("Gf", G.at[1, 0], G.at[3, 0], yp)
    for i in (0, 3):
        reg("O%d" % i, O.at[i, 1], SB.at[i], sib)
    for i in (1, 2):
        for h in (0, 1):
            piece = pl.ds(h * HT, HT)
            reg("O%d%d" % (i, h), O.at[i, 1, :, piece], SB.at[i, :, piece], sib)

    def ring4(tag, a, b, r, plus, minus):
        reg(tag + "0", a(2), r(0), plus)
        reg(tag + "1", b(2), r(1), minus)
        reg(tag + "2", b(1), r(2), plus)
        reg(tag + "3", a(-1), r(3), minus)
        reg(tag + "4", a(1), r(4), plus)
        reg(tag + "5", b(-1), r(5), minus)

        def mid():
            recv(tag + "0")
            add_rows(a(1), [r(0)])
            start(tag + "4")
            recv(tag + "1")
            add_rows(b(-1), [r(1)])
            start(tag + "5")

        return mid

    def ring8(tag, a, b, full, rh, r, plus, minus):
        reg(tag + "0", a(4), rh(0), plus)
        reg(tag + "1", b(4), rh(1), minus)
        for s, k in ((0, 3), (1, 2), (2, 1)):
            reg(tag + "p%d" % k, full(k), r(2 * s), plus)
            reg(tag + "m%d" % k, full(-k), r(2 * s + 1), minus)

        def hop(k):
            if k == 3:
                recv(tag + "0")
                add_rows(a(3), [rh(0)])
                start(tag + "p3")
                recv(tag + "1")
                add_rows(b(-3), [rh(1)])
                start(tag + "m3")
                return
            s = 2 - k
            recv(tag + "p%d" % (k + 1))
            add_rows(full(k), [r(2 * s)])
            start(tag + "p%d" % k)
            recv(tag + "m%d" % (k + 1))
            add_rows(full(-k), [r(2 * s + 1)])
            start(tag + "m%d" % k)

        return hop

    slot_of = {0: 0, -1: 1, 1: 2, 2: 3}
    y_mid = []
    for p in (0, 1):
        piece = pl.ds(p * HT, HT)
        y_mid.append(ring4(
            "y%d" % p,
            lambda k, piece=piece: O.at[slot_of[k], 0, 0, piece],
            lambda k, piece=piece: O.at[slot_of[k], 0, 1, piece],
            lambda i, piece=piece: RY.at[i, piece],
            yp, ym,
        ))

    hz = NZ // 2
    rows = S1.shape[3]
    hr = rows // 2
    s1_mid, s1_hop = [], []
    for c, tag in ((0, "s1a"), (1, "s1b")):
        s1_mid.append(ring4(
            tag + "x",
            lambda k, c=c: S1.at[c, at_x(k), pl.ds(0, hz)],
            lambda k, c=c: S1.at[c, at_x(k), pl.ds(hz, hz)],
            lambda i, c=c: R1.at[c, i], xp, xm,
        ))
        s1_hop.append(ring8(
            tag + "z",
            lambda k, c=c: S1.at[c, x, at_z(k), pl.ds(0, hr)],
            lambda k, c=c: S1.at[c, x, at_z(k), pl.ds(hr, hr)],
            lambda k, c=c: S1.at[c, x, at_z(k)],
            lambda i, c=c: R1h.at[c, i], lambda i, c=c: R1z.at[c, i], zp, zm,
        ))

    def s1_turn(c):
        tag = ("s1a", "s1b")[c]
        recv(tag + "x3", tag + "x4")
        add_rows(S1.at[c, x, pl.ds(0, hz)], [R1.at[c, 3], R1.at[c, 4]])
        recv(tag + "x2", tag + "x5")
        add_rows(S1.at[c, x, pl.ds(hz, hz)], [R1.at[c, 2], R1.at[c, 5]])
        start(tag + "z0", tag + "z1")

    hx = NX // 2
    f2 = lambda k: S2.at[at_z(k)]
    s2_hop = ring8(
        "s2z",
        lambda k: S2.at[at_z(k), pl.ds(0, hx)],
        lambda k: S2.at[at_z(k), pl.ds(hx, hx)],
        f2, lambda i: R2h.at[i], lambda i: R2z.at[i], zp, zm,
    )
    a2 = lambda k: S2.at[z, at_x(k), pl.ds(0, hr)]
    b2 = lambda k: S2.at[z, at_x(k), pl.ds(hr, hr)]
    s2_mid = ring4("s2x", a2, b2, lambda i: R2x.at[i], xp, xm)

    hd = D // 2
    f3 = lambda k: S3.at[at_z(k)]
    s3_hop = ring8(
        "s3z",
        lambda k: S3.at[at_z(k), :, pl.ds(0, hd)],
        lambda k: S3.at[at_z(k), :, pl.ds(hd, hd)],
        f3, lambda i: R3h.at[i], lambda i: R3z.at[i], zp, zm,
    )
    a3 = lambda k: S3x.at[at_x(k), :, pl.ds(0, hd)]
    b3 = lambda k: S3x.at[at_x(k), :, pl.ds(hd, hd)]
    s3_mid = ring4("s3x", a3, b3, lambda i: R3x.at[i], xp, xm)
    assert len(copies) <= COPIES

    loads = [
        pltpu.make_async_copy(tok.at[pl.ds(0, HT)], X.at[0, 0, 0], load_sem.at[0]),
        pltpu.make_async_copy(cot.at[pl.ds(0, HT)], C.at[0, 0, 0], load_sem.at[1]),
        pltpu.make_async_copy(tok.at[pl.ds(HT, HT)], X.at[0, 1, 0], load_sem.at[2]),
        pltpu.make_async_copy(cot.at[pl.ds(HT, HT)], C.at[0, 1, 0], load_sem.at[3]),
        pltpu.make_async_copy(wg, Wgu.at[:, pl.ds(0, H)], load_sem.at[4]),
        pltpu.make_async_copy(wu, Wgu.at[:, pl.ds(H, H)], load_sem.at[5]),
        pltpu.make_async_copy(wd, Wd, load_sem.at[6]),
    ]
    for cp in loads:
        cp.start()

    barrier = pltpu.get_barrier_semaphore()
    near = (sib, yp, ym, xp, xm, zp, zm)
    for dev in near:
        pl.semaphore_signal(barrier, inc=1, device_id=dev, device_id_type=pl.DeviceIdType.MESH)

    rows16 = lax.broadcasted_iota(jnp.int32, (16, T), 0)
    dense = jnp.zeros((16, T), F32)
    for k in range(ids_t.shape[0]):
        dense = dense + jnp.where(ids_t[k : k + 1, :] == rows16, gates_t[k : k + 1, :].astype(F32), 0.0)
    G[0, 0] = dense.astype(BF16)

    for cp in loads[:4]:
        cp.wait()
    pl.semaphore_wait(barrier, len(near))
    start("Gp", "Gm", "Xp0", "Xm0", "Cp0", "Cm0", "Xp1", "Xm1", "Cp1", "Cm1", "Gs0", "Xs0", "Cs0")

    q = lax.broadcasted_iota(jnp.int32, PT.shape, 0)
    unit = lax.broadcasted_iota(jnp.int32, PT.shape, 1)
    row = ((unit // per) % NZ) * (NX * per) + (unit // (per * NZ)) * per + unit % per
    PT[...] = jnp.where(q == row, 1.0, 0.0).astype(BF16)

    for cp in loads[4:]:
        cp.wait()

    mine = (rows16 == ex).astype(F32).astype(BF16)

    def rows_of(i):
        return pl.ds(pl.multiple_of(i * 2 * T, 2 * T), 2 * T)

    def place(i, p):
        own = (i == 0) | (i == 3)
        return jnp.where(own, i, 1 + p), jnp.where(own, p, i - 1)

    def hidden(i):
        for p in (0, 1):
            slot, half = place(i, p)
            for s in (0, 1):
                GT[p, s] = dot(G[slot, s], mine, TN)
                at = (p * 2 + s) * HT
                GC[at : at + HT, :] = GT[p, s, pl.ds(pl.multiple_of(half * HT, HT), HT), :]
        gate = GC[:, :1]
        here = rows_of(i)
        inputs = X[i].reshape(2 * T, D)
        out_grad = (C[i].reshape(2 * T, D).astype(F32) * gate).astype(BF16)
        OG[here, :] = out_grad
        pre = dot(inputs, Wgu[...])
        act_grad = dot(out_grad, Wd[...], NT)
        pre_gate, pre_up = pre[:, :H], pre[:, H:]
        sig = 1.0 / (1.0 + jnp.exp(-pre_gate))
        silu = pre_gate * sig
        activated = (silu * pre_up).astype(BF16)
        ACT[...] = activated
        PG[here, H:] = (act_grad * silu).astype(BF16)
        PG[here, :H] = (act_grad * pre_up * sig * (1.0 + pre_gate * (1.0 - sig))).astype(BF16)
        APT[:, here] = dot(PT[...], activated, NT).astype(BF16)

    def outputs(i):
        @pl.loop(0, D // 512)
        def _(n):
            cols = pl.ds(pl.multiple_of(n * 512, 512), 512)
            part = (dot(ACT[...], Wd[:, cols]) * GC[:, :1]).astype(BF16)
            grad = dot(PG[rows_of(i), :], Wgu[cols, :], NT).astype(BF16)
            for p in (0, 1):
                slot, half = place(i, p)
                to = pl.ds(pl.multiple_of(half * HT, HT), HT)
                for s in (0, 1):
                    at = (p * 2 + s) * HT
                    O[slot, s, 0, to, cols] = part[at : at + HT]
                    O[slot, s, 1, to, cols] = grad[at : at + HT]

    def gate_up_part(m, first, count):
        cols = pl.ds(pl.multiple_of(m * 256, 256), 256)
        span = pl.ds(first * 2 * T, count * 2 * T)
        return dot(X[pl.ds(first, count), :, :, :, cols].reshape(count * 2 * T, 256), PG[span, :], TN)

    def down_part(n, first, count):
        cols = pl.ds(pl.multiple_of(n * 512, 512), 512)
        span = pl.ds(first * 2 * T, count * 2 * T)
        return dot(APT[:, span], OG[span, cols])

    def partial(first, count, fresh):
        @pl.loop(0, D // 256)
        def _(m):
            here = pl.ds(pl.multiple_of(m * 256, 256), 256)
            new = gate_up_part(m, first, count)
            GACC[here, :] = new if fresh else GACC[here, :] + new

        @pl.loop(0, D // 512)
        def _(n):
            cols = pl.ds(pl.multiple_of(n * 512, 512), 512)
            new = down_part(n, first, count)
            DACC[:, cols] = new if fresh else DACC[:, cols] + new

    def finish():
        @pl.loop(0, D // 512)
        def _(n):
            cols = pl.ds(pl.multiple_of(n * 512, 512), 512)
            S3[:, :, cols] = (DACC[:, cols] + down_part(n, 3, 1)).astype(BF16).reshape(NZ, NX * per, 512)

        start("s3z0", "s3z1")

        @pl.loop(0, 8)
        def _(t):
            k = t // 2
            xx = (x + jnp.where(k == 0, 2, jnp.where(k == 1, 1, jnp.where(k == 2, 3, 0)))) % NX
            half = t % 2
            m = xx * 2 + half
            here = pl.ds(pl.multiple_of(m * 256, 256), 256)
            new = (GACC[here, :] + gate_up_part(m, 3, 1)).astype(BF16)
            for c in (0, 1):
                S1[c, xx, pl.ds(half * hz, hz)] = new[:, c * (CX // 2) : (c + 1) * (CX // 2)].reshape(hz, rows, CX // 2)
            S2[pl.ds(half * hz, hz), xx] = new[:, CX:].reshape(hz, rows, 2 * H - CX)
            for at, name in ((0, "x0"), (1, "x1"), (3, "x2"), (4, "x3")):
                @pl.when(t == at)
                def _():
                    start("s1a" + name, "s1b" + name)

        start("s2z0", "s2z1")

    def fold(i):
        recv("O%d" % i)
        for a in (0, 1):
            add_rows(O.at[i, 0, a], [SB.at[i, a]])

    def fold_half(h):
        piece = pl.ds(h * HT, HT)
        for i in (1, 2):
            recv("O%d%d" % (i, h))
            for a in (0, 1):
                add_rows(O.at[i, 0, a, piece], [SB.at[i, a, piece]])
        start("y%d3" % h, "y%d2" % h)

    def step(i, carry):
        @pl.when(i == 0)
        def _():
            recv("Xs0", "Cs0", "Gs0")

        @pl.when(i == 1)
        def _():
            partial(0, 1, True)
            recv("Gp", "Gm")
            start("Gs1", "Gs2", "Gf")
            recv("Xp0", "Cp0")
            start("Xf0", "Cf0")
            recv("Xm0", "Cm0")
            start("Xs1", "Cs1")
            recv("Gs1", "Gs2", "Xs1", "Cs1")

        @pl.when(i == 2)
        def _():
            partial(1, 1, False)
            recv("Gf")
            start("Gs3")
            recv("Xm1", "Cm1")
            start("Xf1", "Cf1")
            recv("Xp1", "Cp1")
            start("Xs2", "Cs2")
            fold_half(0)
            recv("Xs2", "Cs2")

        @pl.when(i == 3)
        def _():
            partial(2, 1, False)
            fold_half(1)
            fold(0)
            recv("Xf0", "Cf0", "Xf1", "Cf1")
            start("Xs3", "Cs3")
            recv("Gs3", "Xs3", "Cs3")

        hidden(i)

        @pl.when(i == 3)
        def _():
            finish()

        outputs(i)
        for k, names in ((0, ("O0",)), (1, ("O10", "O20")), (2, ("O11", "O21")), (3, ("O3",))):
            @pl.when(i == k)
            def _():
                start(*names)
        return carry

    lax.fori_loop(0, 4, step, 0)

    def y_final(p):
        recv("y%d2" % p, "y%d3" % p, "y%d4" % p, "y%d5" % p)

        @pl.loop(0, HT // 16)
        def _(i):
            sl = pl.ds(pl.multiple_of(p * HT + i * 16, 16), 16)
            mixed[sl, :] = (
                O[0, 0, 0, sl, :].astype(F32) + RY[3, sl, :].astype(F32) + RY[4, sl, :].astype(F32)
            ).astype(BF16)
            gtok[sl, :] = (
                O[0, 0, 1, sl, :].astype(F32) + RY[2, sl, :].astype(F32) + RY[5, sl, :].astype(F32)
            ).astype(BF16)

    def s3_turn():
        recv("s3zp1", "s3zm1")
        p_row = lax.broadcasted_iota(jnp.int32, (NX * 16, NX * per), 0)
        p_unit = lax.broadcasted_iota(jnp.int32, (NX * 16, NX * per), 1)
        apart = jnp.where(p_row == (p_unit // per) * 16 + p_unit % per, 1.0, 0.0).astype(BF16)

        @pl.loop(0, D // 512)
        def _(n):
            cols = pl.ds(pl.multiple_of(n * 512, 512), 512)
            total = S3[z, :, cols].astype(F32) + R3z[4, :, cols].astype(F32) + R3z[5, :, cols].astype(F32)
            S3x[:, :, cols] = dot(apart, total.astype(BF16)).astype(BF16).reshape(NX, 16, 512)

        start("s3x0", "s3x1", "s3x2", "s3x3")

    def s2_turn():
        recv("s2zp1", "s2zm1")
        add_rows(f2(0), [R2z.at[4], R2z.at[5]])
        start("s2x0", "s2x1", "s2x2", "s2x3")

    def s3_end():
        recv("s3x2", "s3x3", "s3x4", "s3x5")
        low = a3(0)[...].astype(F32) + R3x[3].astype(F32) + R3x[4].astype(F32)
        high = b3(0)[...].astype(F32) + R3x[2].astype(F32) + R3x[5].astype(F32)
        for j in range(per):
            gdown[j, :, :hd] = low[j : j + 1]
            gdown[j, :, hd:] = high[j : j + 1]

    def s2_end():
        recv("s2x2", "s2x3", "s2x4", "s2x5")
        gup[:hr, CX - H :] = a2(0)[...].astype(F32) + R2x[3].astype(F32) + R2x[4].astype(F32)
        gup[hr:, CX - H :] = b2(0)[...].astype(F32) + R2x[2].astype(F32) + R2x[5].astype(F32)

    def s1_end(c):
        tag = ("s1a", "s1b")[c]
        recv(tag + "zp1", tag + "zm1")
        total = S1[c, x, z].astype(F32) + R1z[c, 4].astype(F32) + R1z[c, 5].astype(F32)
        if c == 0:
            ggate[:, : CX // 2] = total
        else:
            ggate[:, CX // 2 :] = total[:, : H - CX // 2]
            gup[:, : CX - H] = total[:, H - CX // 2 :]

    s3_hop(3)
    s2_hop(3)
    fold(3)
    start("y00", "y01", "y10", "y11")
    s1_mid[0]()
    s1_mid[1]()
    s3_hop(2)
    s2_hop(2)
    s1_turn(0)
    s3_hop(1)
    s1_turn(1)
    y_mid[0]()
    s2_hop(1)
    y_mid[1]()
    s1_hop[0](3)
    s3_turn()
    s1_hop[1](3)
    s2_turn()
    s1_hop[0](2)
    s3_mid()
    s1_hop[1](2)
    y_final(0)
    s2_mid()
    s1_hop[0](1)
    s3_end()
    s1_hop[1](1)
    s2_end()
    y_final(1)
    s1_end(0)
    s1_end(1)

    for n in copies:
        desc(n).wait_send()


def copy_kernel(*refs):
    half = len(refs) // 2
    for k in range(half):
        refs[half + k][...] = refs[k][...]


def per_device(tokens, expert_ids, gates, w_gate, w_up, w_down, cotangent):
    T, D = tokens.shape
    H = w_gate.shape[2]
    rows = D // (NX * NZ)
    per = H // (NX * NZ)
    hbm = pl.BlockSpec(memory_space=pl.ANY)
    vmem = pl.BlockSpec(memory_space=pltpu.VMEM)
    V = pltpu.VMEM
    CX = 512
    CZ = 2 * H - CX
    flops = 2 * 8 * T * D * H * 9
    shapes = (
        jax.ShapeDtypeStruct((T, D), BF16),
        jax.ShapeDtypeStruct((T, D), BF16),
        jax.ShapeDtypeStruct((rows, H), F32),
        jax.ShapeDtypeStruct((rows, H), F32),
        jax.ShapeDtypeStruct((per, 1, D), F32),
    )
    outs = pl.pallas_call(
        moe_kernel,
        out_shape=shapes,
        in_specs=[hbm, hbm, vmem, vmem, hbm, hbm, hbm],
        out_specs=(vmem,) * 5,
        scratch_shapes=[
            V((4, 2, 2, T // 2, D), BF16),
            V((4, 2, 2, T // 2, D), BF16),
            V((4, 2, 16, T), BF16),
            V((2, 2, T, 128), F32),
            V((8 * T, D), BF16),
            V((D, 2 * H), BF16),
            V((H, D), BF16),
            V((4, 2, 2, T, D), BF16),
            V((4, 2, T, D), BF16),
            V((6, T, D), BF16),
            V((8 * T, 2 * H), BF16),
            V((2 * T, H), BF16),
            V((2 * T, 128), F32),
            V((H, 8 * T), BF16),
            V((H, H), BF16),
            V((D, 2 * H), F32),
            V((H, D), F32),
            V((2, NX, NZ, rows, CX // 2), BF16),
            V((NZ, NX, rows, CZ), BF16),
            V((NZ, NX * per, D), BF16),
            V((NX, 16, D), BF16),
            V((2, 6, NZ // 2, rows, CX // 2), BF16),
            V((2, 2, rows // 2, CX // 2), BF16),
            V((2, 6, rows, CX // 2), BF16),
            V((2, NX // 2, rows, CZ), BF16),
            V((6, NX, rows, CZ), BF16),
            V((6, rows // 2, CZ), BF16),
            V((2, NX * per, D // 2), BF16),
            V((6, NX * per, D), BF16),
            V((6, 16, D // 2), BF16),
            pltpu.SemaphoreType.DMA((7,)),
            pltpu.SemaphoreType.DMA((COPIES,)),
            pltpu.SemaphoreType.DMA((COPIES,)),
        ],
        compiler_params=pltpu.CompilerParams(
            collective_id=0, has_side_effects=True, vmem_limit_bytes=63 * 2**20
        ),
        cost_estimate=pl.CostEstimate(flops=flops, bytes_accessed=32 << 20, transcendentals=8 * T * H),
        name="moe",
    )(tokens, cotangent, expert_ids.T, gates.T, w_gate[0], w_up[0], w_down[0])
    mixed, gtok, ggate, gup, gdown = pl.pallas_call(
        copy_kernel,
        out_shape=shapes,
        in_specs=[vmem] * 5,
        out_specs=(vmem,) * 5,
        name="hand_out",
    )(*outs)
    return mixed, gtok, ggate[None], gup[None], gdown.reshape(1, per, D)


def solution(mesh):
    return jax.shard_map(
        per_device,
        mesh=mesh,
        in_specs=(
            P(("dp", "expert"), None),
            P(("dp", "expert"), None),
            P(("dp", "expert"), None),
            P("expert", None, None),
            P("expert", None, None),
            P("expert", None, None),
            P(("dp", "expert"), None),
        ),
        out_specs=(
            P(("dp", "expert"), None),
            P(("dp", "expert"), None),
            P("expert", "dp", None),
            P("expert", "dp", None),
            P("expert", "dp", None),
        ),
        check_vma=False,
    )
```

```python
import functools

import jax
import jax.numpy as jnp
from jax import lax
from jax.experimental import pallas as pl
from jax.experimental.pallas import tpu as pltpu
from jax.sharding import PartitionSpec as P

NX, NZ, NY = 4, 8, 4
F32 = jnp.float32
BF16 = jnp.bfloat16
NN = (((1,), (0,)), ((), ()))
NT = (((1,), (1,)), ((), ()))
TN = (((0,), (0,)), ((), ()))
COPIES = 112


def dot(a, b, dims=NN):
    return lax.dot_general(a, b, dims, preferred_element_type=F32)


def add_rows(dst, srcs):
    rows = dst.shape[-2]
    step = 16 if rows % 16 == 0 else rows

    if len(dst.shape) == 2:
        @pl.loop(0, rows // step)
        def _(i):
            sl = pl.ds(pl.multiple_of(i * step, step), step)
            total = dst[sl, :].astype(F32)
            for s in srcs:
                total = total + s[sl, :].astype(F32)
            dst[sl, :] = total.astype(dst.dtype)
    else:
        @pl.loop(0, dst.shape[0])
        def _(i):
            total = dst[i].astype(F32)
            for s in srcs:
                total = total + s[i].astype(F32)
            dst[i] = total.astype(dst.dtype)


def moe_kernel(
    tok, cot, ids_t, gates_t, wg, wu, wd,
    mixed, gtok, ggate, gup, gdown,
    X, C, G, GT, OG, Wgu, Wd, O, SB, RY, PG, ACT, SILU, SLOPE, GC, APT, PT, GACC, DACC,
    S1, S2, S3, S3x, R1, R1h, R1z, R2h, R2z, R2x, R3h, R3z, R3x,
    load_sem, send_sem, recv_sem,
):
    T, D = tok.shape
    H = wg.shape[1]
    CX = 2 * S1.shape[4]
    per = H // (NX * NZ)
    dp = lax.axis_index("dp")
    ex = lax.axis_index("expert")
    x, z = dp // NZ, dp % NZ
    y, core = ex // 2, ex % 2
    sib = (dp, y * 2 + (1 - core))
    yp = (dp, ((y + 1) % NY) * 2 + core)
    ym = (dp, ((y + NY - 1) % NY) * 2 + core)
    xp = (((x + 1) % NX) * NZ + z, ex)
    xm = (((x + NX - 1) % NX) * NZ + z, ex)
    zp = (x * NZ + (z + 1) % NZ, ex)
    zm = (x * NZ + (z + NZ - 1) % NZ, ex)
    at_x = lambda k: (x + k + NX) % NX
    at_z = lambda k: (z + k + NZ) % NZ

    copies = {}

    def reg(name, src, dst, dev):
        copies[name] = (len(copies), src, dst, dev)

    def desc(name):
        k, src, dst, dev = copies[name]
        return pltpu.make_async_remote_copy(
            src_ref=src, dst_ref=dst, send_sem=send_sem.at[k], recv_sem=recv_sem.at[k],
            device_id=dev, device_id_type=pl.DeviceIdType.MESH,
        )

    def start(*names):
        for n in names:
            desc(n).start()

    def recv(*names):
        for n in names:
            desc(n).wait_recv()

    HT = T // 2
    for nm, buf in (("X", X), ("C", C)):
        for i in range(3):
            reg(nm + "s%d" % i, buf.at[i, :, 0], buf.at[i, :, 1], sib)
        for h in (0, 1):
            reg(nm + "s3%d" % h, buf.at[3, h, 0], buf.at[3, h, 1], sib)
        for h in (0, 1):
            reg(nm + "p%d" % h, buf.at[0, h, 0], buf.at[1 + h, 0, 0], yp)
            reg(nm + "m%d" % h, buf.at[0, h, 0], buf.at[1 + h, 1, 0], ym)
        reg(nm + "f0", buf.at[1, 0, 0], buf.at[3, 0, 0], yp)
        reg(nm + "f1", buf.at[2, 1, 0], buf.at[3, 1, 0], ym)
    for i in range(4):
        reg("Gs%d" % i, G.at[i, 0], G.at[i, 1], sib)
    reg("Gp", G.at[0, 0], G.at[1, 0], yp)
    reg("Gm", G.at[0, 0], G.at[2, 0], ym)
    reg("Gf", G.at[1, 0], G.at[3, 0], yp)
    reg("O0", O.at[0, 1], SB.at[0], sib)
    for a in (0, 1):
        reg("O3%d" % a, O.at[3, 1, a], SB.at[3, a], sib)
    for i in (1, 2):
        for h in (0, 1):
            piece = pl.ds(h * HT, HT)
            reg("O%d%d" % (i, h), O.at[i, 1, :, piece], SB.at[i, :, piece], sib)

    def ring4(tag, a, b, r, plus, minus):
        reg(tag + "0", a(2), r(0), plus)
        reg(tag + "1", b(2), r(1), minus)
        reg(tag + "2", b(1), r(2), plus)
        reg(tag + "3", a(-1), r(3), minus)
        reg(tag + "4", a(1), r(4), plus)
        reg(tag + "5", b(-1), r(5), minus)

        def mid():
            recv(tag + "0")
            add_rows(a(1), [r(0)])
            start(tag + "4")
            recv(tag + "1")
            add_rows(b(-1), [r(1)])
            start(tag + "5")

        return mid

    def ring8(tag, a, b, full, rh, r, plus, minus):
        reg(tag + "0", a(4), rh(0), plus)
        reg(tag + "1", b(4), rh(1), minus)
        for s, k in ((0, 3), (1, 2), (2, 1)):
            reg(tag + "p%d" % k, full(k), r(2 * s), plus)
            reg(tag + "m%d" % k, full(-k), r(2 * s + 1), minus)

        def hop(k):
            if k == 3:
                recv(tag + "0")
                add_rows(a(3), [rh(0)])
                start(tag + "p3")
                recv(tag + "1")
                add_rows(b(-3), [rh(1)])
                start(tag + "m3")
                return
            s = 2 - k
            recv(tag + "p%d" % (k + 1))
            add_rows(full(k), [r(2 * s)])
            start(tag + "p%d" % k)
            recv(tag + "m%d" % (k + 1))
            add_rows(full(-k), [r(2 * s + 1)])
            start(tag + "m%d" % k)

        return hop

    slot_of = {0: 0, -1: 1, 1: 2, 2: 3}
    y_mid = []
    for p in (0, 1):
        piece = pl.ds(p * HT, HT)
        y_mid.append(ring4(
            "y%d" % p,
            lambda k, piece=piece: O.at[slot_of[k], 0, 0, piece],
            lambda k, piece=piece: O.at[slot_of[k], 0, 1, piece],
            lambda i, piece=piece: RY.at[i, piece],
            yp, ym,
        ))

    hz = NZ // 2
    rows = S1.shape[3]
    hr = rows // 2
    s1_mid, s1_hop = [], []
    for c, tag in ((0, "s1a"), (1, "s1b")):
        s1_mid.append(ring4(
            tag + "x",
            lambda k, c=c: S1.at[c, at_x(k), pl.ds(0, hz)],
            lambda k, c=c: S1.at[c, at_x(k), pl.ds(hz, hz)],
            lambda i, c=c: R1.at[c, i], xp, xm,
        ))
        s1_hop.append(ring8(
            tag + "z",
            lambda k, c=c: S1.at[c, x, at_z(k), pl.ds(0, hr)],
            lambda k, c=c: S1.at[c, x, at_z(k), pl.ds(hr, hr)],
            lambda k, c=c: S1.at[c, x, at_z(k)],
            lambda i, c=c: R1h.at[c, i], lambda i, c=c: R1z.at[c, i], zp, zm,
        ))

    def s1_turn(c):
        tag = ("s1a", "s1b")[c]
        recv(tag + "x3", tag + "x4")
        add_rows(S1.at[c, x, pl.ds(0, hz)], [R1.at[c, 3], R1.at[c, 4]])
        recv(tag + "x2", tag + "x5")
        add_rows(S1.at[c, x, pl.ds(hz, hz)], [R1.at[c, 2], R1.at[c, 5]])
        start(tag + "z0", tag + "z1")

    hx = NX // 2
    f2 = lambda k: S2.at[at_z(k)]
    s2_hop = ring8(
        "s2z",
        lambda k: S2.at[at_z(k), pl.ds(0, hx)],
        lambda k: S2.at[at_z(k), pl.ds(hx, hx)],
        f2, lambda i: R2h.at[i], lambda i: R2z.at[i], zp, zm,
    )
    a2 = lambda k: S2.at[z, at_x(k), pl.ds(0, hr)]
    b2 = lambda k: S2.at[z, at_x(k), pl.ds(hr, hr)]
    s2_mid = ring4("s2x", a2, b2, lambda i: R2x.at[i], xp, xm)

    hd = D // 2
    f3 = lambda k: S3.at[at_z(k)]
    s3_hop = ring8(
        "s3z",
        lambda k: S3.at[at_z(k), :, pl.ds(0, hd)],
        lambda k: S3.at[at_z(k), :, pl.ds(hd, hd)],
        f3, lambda i: R3h.at[i], lambda i: R3z.at[i], zp, zm,
    )
    a3 = lambda k: S3x.at[at_x(k), :, pl.ds(0, hd)]
    b3 = lambda k: S3x.at[at_x(k), :, pl.ds(hd, hd)]
    s3_mid = ring4("s3x", a3, b3, lambda i: R3x.at[i], xp, xm)
    assert len(copies) <= COPIES

    barrier = pltpu.get_barrier_semaphore()
    near = (sib, yp, ym, xp, xm, zp, zm)
    for dev in near:
        pl.semaphore_signal(barrier, inc=1, device_id=dev, device_id_type=pl.DeviceIdType.MESH)

    loads = [
        pltpu.make_async_copy(tok.at[pl.ds(0, HT)], X.at[0, 0, 0], load_sem.at[0]),
        pltpu.make_async_copy(cot.at[pl.ds(0, HT)], C.at[0, 0, 0], load_sem.at[1]),
        pltpu.make_async_copy(tok.at[pl.ds(HT, HT)], X.at[0, 1, 0], load_sem.at[2]),
        pltpu.make_async_copy(cot.at[pl.ds(HT, HT)], C.at[0, 1, 0], load_sem.at[3]),
        pltpu.make_async_copy(wg, Wgu.at[:, pl.ds(0, H)], load_sem.at[4]),
        pltpu.make_async_copy(wu, Wgu.at[:, pl.ds(H, H)], load_sem.at[5]),
        pltpu.make_async_copy(wd, Wd, load_sem.at[6]),
    ]
    for cp in loads:
        cp.start()

    rows16 = lax.broadcasted_iota(jnp.int32, (16, T), 0)
    dense = jnp.zeros((16, T), F32)
    for k in range(ids_t.shape[0]):
        dense = dense + jnp.where(ids_t[k : k + 1, :] == rows16, gates_t[k : k + 1, :].astype(F32), 0.0)
    G[0, 0] = dense.astype(BF16)

    for cp in loads[:4]:
        cp.wait()
    pl.semaphore_wait(barrier, len(near))
    start("Gp", "Gm", "Xp0", "Xm0", "Cp0", "Cm0", "Xp1", "Xm1", "Cp1", "Cm1", "Gs0", "Xs0", "Cs0")

    q = lax.broadcasted_iota(jnp.int32, PT.shape, 0)
    unit = lax.broadcasted_iota(jnp.int32, PT.shape, 1)
    row = ((unit // per) % NZ) * (NX * per) + (unit // (per * NZ)) * per + unit % per
    PT[...] = jnp.where(q == row, 1.0, 0.0).astype(BF16)

    for cp in loads[4:]:
        cp.wait()

    mine = (rows16 == ex).astype(F32).astype(BF16)

    def rows_of(i):
        return pl.ds(pl.multiple_of(i * 2 * T, 2 * T), 2 * T)

    def place(i, p):
        own = (i == 0) | (i == 3)
        return jnp.where(own, i, 1 + p), jnp.where(own, p, i - 1)

    def from_tokens(i):
        for p in (0, 1):
            slot, half = place(i, p)
            for s in (0, 1):
                GT[p, s] = dot(G[slot, s], mine, TN)
                at = (p * 2 + s) * HT
                GC[at : at + HT, :] = GT[p, s, pl.ds(pl.multiple_of(half * HT, HT), HT), :]
        pre = dot(X[i].reshape(2 * T, D), Wgu[...])
        pre_gate, pre_up = pre[:, :H], pre[:, H:]
        sig = 1.0 / (1.0 + jnp.exp(-pre_gate))
        silu = pre_gate * sig
        activated = (silu * pre_up).astype(BF16)
        ACT[...] = activated
        SILU[...] = silu
        SLOPE[...] = pre_up * sig * (1.0 + pre_gate * (1.0 - sig))
        APT[:, rows_of(i)] = dot(PT[...], activated, NT).astype(BF16)
        store(i, 0, lambda cols: dot(ACT[...], Wd[:, cols]) * GC[:, :1])

    def from_cotangents(i):
        here = rows_of(i)
        out_grad = (C[i].reshape(2 * T, D).astype(F32) * GC[:, :1]).astype(BF16)
        OG[here, :] = out_grad
        act_grad = dot(out_grad, Wd[...], NT)
        PG[here, H:] = (act_grad * SILU[...]).astype(BF16)
        PG[here, :H] = (act_grad * SLOPE[...]).astype(BF16)

    def token_grads(i):
        store(i, 1, lambda cols: dot(PG[rows_of(i), :], Wgu[cols, :], NT))

    def store(i, a, value):
        @pl.loop(0, D // 1024)
        def _(n):
            cols = pl.ds(pl.multiple_of(n * 1024, 1024), 1024)
            result = value(cols).astype(BF16)
            for p in (0, 1):
                slot, half = place(i, p)
                to = pl.ds(pl.multiple_of(half * HT, HT), HT)
                for s in (0, 1):
                    at = (p * 2 + s) * HT
                    O[slot, s, a, to, cols] = result[at : at + HT]

    TILE = D // NX

    def gate_up_part(m, first, count):
        cols = pl.ds(pl.multiple_of(m * TILE, TILE), TILE)
        span = pl.ds(first * 2 * T, count * 2 * T)
        return dot(X[pl.ds(first, count), :, :, :, cols].reshape(count * 2 * T, TILE), PG[span, :], TN)

    def down_part(n, first, count):
        cols = pl.ds(pl.multiple_of(n * 1024, 1024), 1024)
        span = pl.ds(first * 2 * T, count * 2 * T)
        return dot(APT[:, span], OG[span, cols])

    def partial(first, count, fresh):
        @pl.loop(0, NX)
        def _(m):
            here = pl.ds(pl.multiple_of(m * TILE, TILE), TILE)
            new = gate_up_part(m, first, count)
            GACC[here, :] = new if fresh else GACC[here, :] + new

        @pl.loop(0, D // 1024)
        def _(n):
            cols = pl.ds(pl.multiple_of(n * 1024, 1024), 1024)
            new = down_part(n, first, count)
            DACC[:, cols] = new if fresh else DACC[:, cols] + new

    def finish():
        @pl.loop(0, D // 1024)
        def _(n):
            cols = pl.ds(pl.multiple_of(n * 1024, 1024), 1024)
            S3[:, :, cols] = (DACC[:, cols] + down_part(n, 3, 1)).astype(BF16).reshape(NZ, NX * per, 1024)

        start("s3z0", "s3z1")

        @pl.loop(0, NX)
        def _(k):
            xx = (x + jnp.where(k == 0, 2, jnp.where(k == 1, 1, jnp.where(k == 2, 3, 0)))) % NX
            here = pl.ds(pl.multiple_of(xx * TILE, TILE), TILE)
            new = (GACC[here, :] + gate_up_part(xx, 3, 1)).astype(BF16)
            for c in (0, 1):
                S1[c, xx] = new[:, c * (CX // 2) : (c + 1) * (CX // 2)].reshape(NZ, rows, CX // 2)
            S2[:, xx] = new[:, CX:].reshape(NZ, rows, 2 * H - CX)
            for at, names in ((0, ("x0", "x1")), (1, ("x2",)), (2, ("x3",))):
                @pl.when(k == at)
                def _():
                    for name in names:
                        start("s1a" + name, "s1b" + name)

        start("s2z0", "s2z1")

    def fold_own():
        recv("O0")
        for a in (0, 1):
            add_rows(O.at[0, 0, a], [SB.at[0, a]])

    def fold_far(a):
        recv("O3%d" % a)
        add_rows(O.at[3, 0, a], [SB.at[3, a]])
        start("y0%d" % a, "y1%d" % a)

    def fold_half(h):
        piece = pl.ds(h * HT, HT)
        for i in (1, 2):
            recv("O%d%d" % (i, h))
            for a in (0, 1):
                add_rows(O.at[i, 0, a, piece], [SB.at[i, a, piece]])
        start("y%d3" % h, "y%d2" % h)

    def step(i, carry):
        @pl.when(i == 0)
        def _():
            recv("Xs0", "Cs0", "Gs0")

        @pl.when(i == 1)
        def _():
            partial(0, 1, True)
            recv("Gp", "Gm")
            start("Gs1", "Gs2", "Gf")
            recv("Xp0", "Cp0")
            start("Xf0", "Cf0")
            recv("Xm0", "Cm0")
            start("Xs1", "Cs1")
            recv("Gs1", "Gs2", "Xs1", "Cs1")

        @pl.when(i == 2)
        def _():
            partial(1, 1, False)
            recv("Gf")
            start("Gs3")
            recv("Xm1", "Cm1")
            start("Xf1", "Cf1")
            recv("Xp1", "Cp1")
            start("Xs2", "Cs2")
            fold_half(0)
            recv("Xs2", "Cs2")

        @pl.when(i == 3)
        def _():
            recv("Xf0")
            start("Xs30")
            recv("Xf1")
            start("Xs31")
            partial(2, 1, False)
            recv("Gs3", "Xs30", "Xs31")

        from_tokens(i)

        @pl.when(i == 3)
        def _():
            start("O30")
            recv("Cf0")
            start("Cs30")
            recv("Cf1")
            start("Cs31")
            fold_half(1)
            recv("Cs30", "Cs31")

        from_cotangents(i)

        @pl.when(i == 3)
        def _():
            finish()
            fold_far(0)
            fold_own()

        token_grads(i)
        for k, names in ((0, ("O0",)), (1, ("O10", "O20")), (2, ("O11", "O21")), (3, ("O31",))):
            @pl.when(i == k)
            def _():
                start(*names)
        return carry

    lax.fori_loop(0, 4, step, 0)

    def y_final(p):
        recv("y%d2" % p, "y%d3" % p, "y%d4" % p, "y%d5" % p)

        @pl.loop(0, HT // 16)
        def _(i):
            sl = pl.ds(pl.multiple_of(p * HT + i * 16, 16), 16)
            mixed[sl, :] = (
                O[0, 0, 0, sl, :].astype(F32) + RY[3, sl, :].astype(F32) + RY[4, sl, :].astype(F32)
            ).astype(BF16)
            gtok[sl, :] = (
                O[0, 0, 1, sl, :].astype(F32) + RY[2, sl, :].astype(F32) + RY[5, sl, :].astype(F32)
            ).astype(BF16)

    def s3_turn():
        recv("s3zp1", "s3zm1")
        p_row = lax.broadcasted_iota(jnp.int32, (NX * 16, NX * per), 0)
        p_unit = lax.broadcasted_iota(jnp.int32, (NX * 16, NX * per), 1)
        apart = jnp.where(p_row == (p_unit // per) * 16 + p_unit % per, 1.0, 0.0).astype(BF16)

        @pl.loop(0, D // 512)
        def _(n):
            cols = pl.ds(pl.multiple_of(n * 512, 512), 512)
            total = S3[z, :, cols].astype(F32) + R3z[4, :, cols].astype(F32) + R3z[5, :, cols].astype(F32)
            S3x[:, :, cols] = dot(apart, total.astype(BF16)).astype(BF16).reshape(NX, 16, 512)

        start("s3x0", "s3x1", "s3x2", "s3x3")

    def s2_turn():
        recv("s2zp1", "s2zm1")
        add_rows(f2(0), [R2z.at[4], R2z.at[5]])
        start("s2x0", "s2x1", "s2x2", "s2x3")

    def s3_end():
        recv("s3x2", "s3x3", "s3x4", "s3x5")
        low = a3(0)[...].astype(F32) + R3x[3].astype(F32) + R3x[4].astype(F32)
        high = b3(0)[...].astype(F32) + R3x[2].astype(F32) + R3x[5].astype(F32)
        for j in range(per):
            gdown[j, :, :hd] = low[j : j + 1]
            gdown[j, :, hd:] = high[j : j + 1]

    def s2_end():
        recv("s2x2", "s2x3", "s2x4", "s2x5")
        gup[:hr, CX - H :] = a2(0)[...].astype(F32) + R2x[3].astype(F32) + R2x[4].astype(F32)
        gup[hr:, CX - H :] = b2(0)[...].astype(F32) + R2x[2].astype(F32) + R2x[5].astype(F32)

    def s1_end(c):
        tag = ("s1a", "s1b")[c]
        recv(tag + "zp1", tag + "zm1")
        total = S1[c, x, z].astype(F32) + R1z[c, 4].astype(F32) + R1z[c, 5].astype(F32)
        if c == 0:
            ggate[:, : CX // 2] = total
        else:
            ggate[:, CX // 2 :] = total[:, : H - CX // 2]
            gup[:, : CX - H] = total[:, H - CX // 2 :]

    s3_hop(3)
    s2_hop(3)
    fold_far(1)
    s1_mid[0]()
    s3_hop(2)
    s2_hop(2)
    s1_mid[1]()
    s1_turn(0)
    y_mid[0]()
    s3_hop(1)
    s1_turn(1)
    s2_hop(1)
    s1_hop[0](3)
    y_mid[1]()
    s3_turn()
    s1_hop[1](3)
    y_final(0)
    s2_turn()
    s1_hop[0](2)
    s3_mid()
    s1_hop[1](2)
    s2_mid()
    s1_hop[0](1)
    s3_end()
    s1_hop[1](1)
    y_final(1)
    s2_end()
    s1_end(0)
    s1_end(1)

    for n in copies:
        desc(n).wait_send()


def copy_kernel(*refs):
    half = len(refs) // 2
    for k in range(half):
        refs[half + k][...] = refs[k][...]


def per_device(tokens, expert_ids, gates, w_gate, w_up, w_down, cotangent):
    T, D = tokens.shape
    H = w_gate.shape[2]
    rows = D // (NX * NZ)
    per = H // (NX * NZ)
    hbm = pl.BlockSpec(memory_space=pl.ANY)
    vmem = pl.BlockSpec(memory_space=pltpu.VMEM)
    V = pltpu.VMEM
    CX = 512
    CZ = 2 * H - CX
    flops = 2 * 8 * T * D * H * 9
    shapes = (
        jax.ShapeDtypeStruct((T, D), BF16),
        jax.ShapeDtypeStruct((T, D), BF16),
        jax.ShapeDtypeStruct((rows, H), F32),
        jax.ShapeDtypeStruct((rows, H), F32),
        jax.ShapeDtypeStruct((per, 1, D), F32),
    )
    outs = pl.pallas_call(
        moe_kernel,
        out_shape=shapes,
        in_specs=[hbm, hbm, vmem, vmem, hbm, hbm, hbm],
        out_specs=(vmem,) * 5,
        scratch_shapes=[
            V((4, 2, 2, T // 2, D), BF16),
            V((4, 2, 2, T // 2, D), BF16),
            V((4, 2, 16, T), BF16),
            V((2, 2, T, 128), F32),
            V((8 * T, D), BF16),
            V((D, 2 * H), BF16),
            V((H, D), BF16),
            V((4, 2, 2, T, D), BF16),
            V((4, 2, T, D), BF16),
            V((6, T, D), BF16),
            V((8 * T, 2 * H), BF16),
            V((2 * T, H), BF16),
            V((2 * T, H), F32),
            V((2 * T, H), F32),
            V((2 * T, 128), F32),
            V((H, 8 * T), BF16),
            V((H, H), BF16),
            V((D, 2 * H), F32),
            V((H, D), F32),
            V((2, NX, NZ, rows, CX // 2), BF16),
            V((NZ, NX, rows, CZ), BF16),
            V((NZ, NX * per, D), BF16),
            V((NX, 16, D), BF16),
            V((2, 6, NZ // 2, rows, CX // 2), BF16),
            V((2, 2, rows // 2, CX // 2), BF16),
            V((2, 6, rows, CX // 2), BF16),
            V((2, NX // 2, rows, CZ), BF16),
            V((6, NX, rows, CZ), BF16),
            V((6, rows // 2, CZ), BF16),
            V((2, NX * per, D // 2), BF16),
            V((6, NX * per, D), BF16),
            V((6, 16, D // 2), BF16),
            pltpu.SemaphoreType.DMA((7,)),
            pltpu.SemaphoreType.DMA((COPIES,)),
            pltpu.SemaphoreType.DMA((COPIES,)),
        ],
        compiler_params=pltpu.CompilerParams(
            collective_id=0, has_side_effects=True, vmem_limit_bytes=63 * 2**20
        ),
        cost_estimate=pl.CostEstimate(flops=flops, bytes_accessed=32 << 20, transcendentals=8 * T * H),
        name="moe",
    )(tokens, cotangent, expert_ids.T, gates.T, w_gate[0], w_up[0], w_down[0])
    mixed, gtok, ggate, gup, gdown = pl.pallas_call(
        copy_kernel,
        out_shape=shapes,
        in_specs=[vmem] * 5,
        out_specs=(vmem,) * 5,
        name="hand_out",
    )(*outs)
    return mixed, gtok, ggate[None], gup[None], gdown.reshape(1, per, D)


def solution(mesh):
    return jax.shard_map(
        per_device,
        mesh=mesh,
        in_specs=(
            P(("dp", "expert"), None),
            P(("dp", "expert"), None),
            P(("dp", "expert"), None),
            P("expert", None, None),
            P("expert", None, None),
            P("expert", None, None),
            P(("dp", "expert"), None),
        ),
        out_specs=(
            P(("dp", "expert"), None),
            P(("dp", "expert"), None),
            P("expert", "dp", None),
            P("expert", "dp", None),
            P("expert", "dp", None),
        ),
        check_vma=False,
    )
```

```python
import functools

import jax
import jax.numpy as jnp
from jax import lax
from jax.experimental import pallas as pl
from jax.experimental.pallas import tpu as pltpu
from jax.sharding import PartitionSpec as P

NX, NZ, NY = 4, 8, 4
F32 = jnp.float32
BF16 = jnp.bfloat16
NN = (((1,), (0,)), ((), ()))
NT = (((1,), (1,)), ((), ()))
TN = (((0,), (0,)), ((), ()))
COPIES = 112


def dot(a, b, dims=NN):
    return lax.dot_general(a, b, dims, preferred_element_type=F32)


def total_of(terms):
    if len(terms) == 2:
        return terms[0] + terms[1]
    total = terms[0].astype(F32)
    for t in terms[1:]:
        total = total + t.astype(F32)
    return total.astype(BF16)


def add_rows(dst, srcs):
    rows = dst.shape[-2]
    step = 16 if rows % 16 == 0 else rows

    if len(dst.shape) == 2:
        @pl.loop(0, rows // step)
        def _(i):
            sl = pl.ds(pl.multiple_of(i * step, step), step)
            dst[sl, :] = total_of([dst[sl, :]] + [s[sl, :] for s in srcs])
    else:
        @pl.loop(0, dst.shape[0])
        def _(i):
            dst[i] = total_of([dst[i]] + [s[i] for s in srcs])


def moe_kernel(
    tok, cot, ids_t, gates_t, wg, wu, wd,
    mixed, gtok, ggate, gup, gdown,
    X, C, G, GT, OG, Wgu, Wd, O, SB, RY, PG, ACT, SILU, SLOPE, GC, APT, PT, GACC, DACC,
    S1, S2, S3, S3x, R1, R1h, R1z, R2h, R2z, R2x, R3h, R3z, R3x,
    load_sem, send_sem, recv_sem,
):
    T, D = tok.shape
    H = wg.shape[1]
    CX = 2 * S1.shape[4]
    per = H // (NX * NZ)
    dp = lax.axis_index("dp")
    ex = lax.axis_index("expert")
    x, z = dp // NZ, dp % NZ
    y, core = ex // 2, ex % 2
    sib = (dp, y * 2 + (1 - core))
    yp = (dp, ((y + 1) % NY) * 2 + core)
    ym = (dp, ((y + NY - 1) % NY) * 2 + core)
    xp = (((x + 1) % NX) * NZ + z, ex)
    xm = (((x + NX - 1) % NX) * NZ + z, ex)
    zp = (x * NZ + (z + 1) % NZ, ex)
    zm = (x * NZ + (z + NZ - 1) % NZ, ex)
    at_x = lambda k: (x + k + NX) % NX
    at_z = lambda k: (z + k + NZ) % NZ

    copies = {}

    def reg(name, src, dst, dev):
        copies[name] = (len(copies), src, dst, dev)

    def desc(name):
        k, src, dst, dev = copies[name]
        return pltpu.make_async_remote_copy(
            src_ref=src, dst_ref=dst, send_sem=send_sem.at[k], recv_sem=recv_sem.at[k],
            device_id=dev, device_id_type=pl.DeviceIdType.MESH,
        )

    def start(*names):
        for n in names:
            desc(n).start()

    def recv(*names):
        for n in names:
            desc(n).wait_recv()

    HT = T // 2
    for nm, buf in (("X", X), ("C", C)):
        for i in range(3):
            reg(nm + "s%d" % i, buf.at[i, :, 0], buf.at[i, :, 1], sib)
        for h in (0, 1):
            reg(nm + "s3%d" % h, buf.at[3, h, 0], buf.at[3, h, 1], sib)
        for h in (0, 1):
            reg(nm + "p%d" % h, buf.at[0, h, 0], buf.at[1 + h, 0, 0], yp)
            reg(nm + "m%d" % h, buf.at[0, h, 0], buf.at[1 + h, 1, 0], ym)
        reg(nm + "f0", buf.at[1, 0, 0], buf.at[3, 0, 0], yp)
        reg(nm + "f1", buf.at[2, 1, 0], buf.at[3, 1, 0], ym)
    for i in range(4):
        reg("Gs%d" % i, G.at[i, 0], G.at[i, 1], sib)
    reg("Gp", G.at[0, 0], G.at[1, 0], yp)
    reg("Gm", G.at[0, 0], G.at[2, 0], ym)
    reg("Gf", G.at[1, 0], G.at[3, 0], yp)
    reg("O0", O.at[0, 1], SB.at[0], sib)
    for a in (0, 1):
        reg("O3%d" % a, O.at[3, 1, a], SB.at[3, a], sib)
    for i in (1, 2):
        for h in (0, 1):
            piece = pl.ds(h * HT, HT)
            reg("O%d%d" % (i, h), O.at[i, 1, :, piece], SB.at[i, :, piece], sib)

    def ring4(tag, a, b, r, plus, minus):
        reg(tag + "0", a(2), r(0), plus)
        reg(tag + "1", b(2), r(1), minus)
        reg(tag + "2", b(1), r(2), plus)
        reg(tag + "3", a(-1), r(3), minus)
        reg(tag + "4", a(1), r(4), plus)
        reg(tag + "5", b(-1), r(5), minus)

        def mid():
            recv(tag + "0")
            add_rows(a(1), [r(0)])
            start(tag + "4")
            recv(tag + "1")
            add_rows(b(-1), [r(1)])
            start(tag + "5")

        return mid

    def ring8(tag, a, b, full, rh, r, plus, minus):
        reg(tag + "0", a(4), rh(0), plus)
        reg(tag + "1", b(4), rh(1), minus)
        for s, k in ((0, 3), (1, 2), (2, 1)):
            reg(tag + "p%d" % k, full(k), r(2 * s), plus)
            reg(tag + "m%d" % k, full(-k), r(2 * s + 1), minus)

        def hop(k):
            if k == 3:
                recv(tag + "0")
                add_rows(a(3), [rh(0)])
                start(tag + "p3")
                recv(tag + "1")
                add_rows(b(-3), [rh(1)])
                start(tag + "m3")
                return
            s = 2 - k
            recv(tag + "p%d" % (k + 1))
            add_rows(full(k), [r(2 * s)])
            start(tag + "p%d" % k)
            recv(tag + "m%d" % (k + 1))
            add_rows(full(-k), [r(2 * s + 1)])
            start(tag + "m%d" % k)

        return hop

    slot_of = {0: 0, -1: 1, 1: 2, 2: 3}
    y_mid = []
    for p in (0, 1):
        piece = pl.ds(p * HT, HT)
        y_mid.append(ring4(
            "y%d" % p,
            lambda k, piece=piece: O.at[slot_of[k], 0, 0, piece],
            lambda k, piece=piece: O.at[slot_of[k], 0, 1, piece],
            lambda i, piece=piece: RY.at[i, piece],
            yp, ym,
        ))

    hz = NZ // 2
    rows = S1.shape[3]
    hr = rows // 2
    s1_mid, s1_hop = [], []
    for c, tag in ((0, "s1a"), (1, "s1b")):
        s1_mid.append(ring4(
            tag + "x",
            lambda k, c=c: S1.at[c, at_x(k), pl.ds(0, hz)],
            lambda k, c=c: S1.at[c, at_x(k), pl.ds(hz, hz)],
            lambda i, c=c: R1.at[c, i], xp, xm,
        ))
        s1_hop.append(ring8(
            tag + "z",
            lambda k, c=c: S1.at[c, x, at_z(k), pl.ds(0, hr)],
            lambda k, c=c: S1.at[c, x, at_z(k), pl.ds(hr, hr)],
            lambda k, c=c: S1.at[c, x, at_z(k)],
            lambda i, c=c: R1h.at[c, i], lambda i, c=c: R1z.at[c, i], zp, zm,
        ))

    def s1_turn(c):
        tag = ("s1a", "s1b")[c]
        recv(tag + "x3", tag + "x4")
        add_rows(S1.at[c, x, pl.ds(0, hz)], [R1.at[c, 3], R1.at[c, 4]])
        recv(tag + "x2", tag + "x5")
        add_rows(S1.at[c, x, pl.ds(hz, hz)], [R1.at[c, 2], R1.at[c, 5]])
        start(tag + "z0", tag + "z1")

    hx = NX // 2
    f2 = lambda k: S2.at[at_z(k)]
    s2_hop = ring8(
        "s2z",
        lambda k: S2.at[at_z(k), pl.ds(0, hx)],
        lambda k: S2.at[at_z(k), pl.ds(hx, hx)],
        f2, lambda i: R2h.at[i], lambda i: R2z.at[i], zp, zm,
    )
    a2 = lambda k: S2.at[z, at_x(k), pl.ds(0, hr)]
    b2 = lambda k: S2.at[z, at_x(k), pl.ds(hr, hr)]
    s2_mid = ring4("s2x", a2, b2, lambda i: R2x.at[i], xp, xm)

    hd = D // 2
    f3 = lambda k: S3.at[at_z(k)]
    s3_hop = ring8(
        "s3z",
        lambda k: S3.at[at_z(k), :, pl.ds(0, hd)],
        lambda k: S3.at[at_z(k), :, pl.ds(hd, hd)],
        f3, lambda i: R3h.at[i], lambda i: R3z.at[i], zp, zm,
    )
    a3 = lambda k: S3x.at[at_x(k), :, pl.ds(0, hd)]
    b3 = lambda k: S3x.at[at_x(k), :, pl.ds(hd, hd)]
    s3_mid = ring4("s3x", a3, b3, lambda i: R3x.at[i], xp, xm)
    assert len(copies) <= COPIES

    barrier = pltpu.get_barrier_semaphore()
    near = (sib, yp, ym, xp, xm, zp, zm)
    for dev in near:
        pl.semaphore_signal(barrier, inc=1, device_id=dev, device_id_type=pl.DeviceIdType.MESH)

    loads = [
        pltpu.make_async_copy(tok.at[pl.ds(0, HT)], X.at[0, 0, 0], load_sem.at[0]),
        pltpu.make_async_copy(cot.at[pl.ds(0, HT)], C.at[0, 0, 0], load_sem.at[1]),
        pltpu.make_async_copy(tok.at[pl.ds(HT, HT)], X.at[0, 1, 0], load_sem.at[2]),
        pltpu.make_async_copy(cot.at[pl.ds(HT, HT)], C.at[0, 1, 0], load_sem.at[3]),
        pltpu.make_async_copy(wg, Wgu.at[:, pl.ds(0, H)], load_sem.at[4]),
        pltpu.make_async_copy(wu, Wgu.at[:, pl.ds(H, H)], load_sem.at[5]),
        pltpu.make_async_copy(wd, Wd, load_sem.at[6]),
    ]
    for cp in loads:
        cp.start()

    rows16 = lax.broadcasted_iota(jnp.int32, (16, T), 0)
    dense = jnp.zeros((16, T), F32)
    for k in range(ids_t.shape[0]):
        dense = dense + jnp.where(ids_t[k : k + 1, :] == rows16, gates_t[k : k + 1, :].astype(F32), 0.0)
    G[0, 0] = dense.astype(BF16)

    for cp in loads[:4]:
        cp.wait()
    pl.semaphore_wait(barrier, len(near))
    start("Gp", "Gm", "Xp0", "Xm0", "Cp0", "Cm0", "Xp1", "Xm1", "Cp1", "Cm1", "Gs0", "Xs0", "Cs0")

    q = lax.broadcasted_iota(jnp.int32, PT.shape, 0)
    unit = lax.broadcasted_iota(jnp.int32, PT.shape, 1)
    row = ((unit // per) % NZ) * (NX * per) + (unit // (per * NZ)) * per + unit % per
    PT[...] = jnp.where(q == row, 1.0, 0.0).astype(BF16)

    for cp in loads[4:]:
        cp.wait()

    mine = (rows16 == ex).astype(F32).astype(BF16)

    def rows_of(i):
        return pl.ds(pl.multiple_of(i * 2 * T, 2 * T), 2 * T)

    def place(i, p):
        own = (i == 0) | (i == 3)
        return jnp.where(own, i, 1 + p), jnp.where(own, p, i - 1)

    def from_tokens(i):
        for p in (0, 1):
            slot, half = place(i, p)
            for s in (0, 1):
                GT[p, s] = dot(G[slot, s], mine, TN)
                at = (p * 2 + s) * HT
                GC[at : at + HT, :] = GT[p, s, pl.ds(pl.multiple_of(half * HT, HT), HT), :]
        pre = dot(X[i].reshape(2 * T, D), Wgu[...])
        pre_gate, pre_up = pre[:, :H], pre[:, H:]
        sig = 1.0 / (1.0 + jnp.exp(-pre_gate))
        silu = pre_gate * sig
        activated = (silu * pre_up).astype(BF16)
        ACT[...] = activated
        SILU[...] = silu
        SLOPE[...] = pre_up * sig * (1.0 + pre_gate * (1.0 - sig))
        APT[:, rows_of(i)] = dot(PT[...], activated, NT).astype(BF16)
        store(i, 0, lambda cols: dot(ACT[...], Wd[:, cols]) * GC[:, :1])

    def from_cotangents(i):
        here = rows_of(i)
        out_grad = (C[i].reshape(2 * T, D).astype(F32) * GC[:, :1]).astype(BF16)
        OG[here, :] = out_grad
        act_grad = dot(out_grad, Wd[...], NT)
        PG[here, H:] = (act_grad * SILU[...]).astype(BF16)
        PG[here, :H] = (act_grad * SLOPE[...]).astype(BF16)

    def token_grads(i):
        store(i, 1, lambda cols: dot(PG[rows_of(i), :], Wgu[cols, :], NT))

    def store(i, a, value):
        @pl.loop(0, D // 1024)
        def _(n):
            cols = pl.ds(pl.multiple_of(n * 1024, 1024), 1024)
            result = value(cols).astype(BF16)
            for p in (0, 1):
                slot, half = place(i, p)
                to = pl.ds(pl.multiple_of(half * HT, HT), HT)
                for s in (0, 1):
                    at = (p * 2 + s) * HT
                    O[slot, s, a, to, cols] = result[at : at + HT]

    TILE = D // NX

    def gate_up_part(m, first, count):
        cols = pl.ds(pl.multiple_of(m * TILE, TILE), TILE)
        span = pl.ds(first * 2 * T, count * 2 * T)
        return dot(X[pl.ds(first, count), :, :, :, cols].reshape(count * 2 * T, TILE), PG[span, :], TN)

    def down_part(n, first, count):
        cols = pl.ds(pl.multiple_of(n * 1024, 1024), 1024)
        span = pl.ds(first * 2 * T, count * 2 * T)
        return dot(APT[:, span], OG[span, cols])

    def partial(first, count, fresh):
        @pl.loop(0, NX)
        def _(m):
            here = pl.ds(pl.multiple_of(m * TILE, TILE), TILE)
            new = gate_up_part(m, first, count)
            GACC[here, :] = new if fresh else GACC[here, :] + new

        @pl.loop(0, D // 1024)
        def _(n):
            cols = pl.ds(pl.multiple_of(n * 1024, 1024), 1024)
            new = down_part(n, first, count)
            DACC[:, cols] = new if fresh else DACC[:, cols] + new

    def finish():
        @pl.loop(0, D // 1024)
        def _(n):
            cols = pl.ds(pl.multiple_of(n * 1024, 1024), 1024)
            S3[:, :, cols] = (DACC[:, cols] + down_part(n, 3, 1)).astype(BF16).reshape(NZ, NX * per, 1024)

        start("s3z0", "s3z1")

        @pl.loop(0, NX)
        def _(k):
            xx = (x + jnp.where(k == 0, 2, jnp.where(k == 1, 1, jnp.where(k == 2, 3, 0)))) % NX
            here = pl.ds(pl.multiple_of(xx * TILE, TILE), TILE)
            new = (GACC[here, :] + gate_up_part(xx, 3, 1)).astype(BF16)
            for c in (0, 1):
                S1[c, xx] = new[:, c * (CX // 2) : (c + 1) * (CX // 2)].reshape(NZ, rows, CX // 2)
            S2[:, xx] = new[:, CX:].reshape(NZ, rows, 2 * H - CX)
            for at, names in ((0, ("x0", "x1")), (1, ("x2",)), (2, ("x3",))):
                @pl.when(k == at)
                def _():
                    for name in names:
                        start("s1a" + name, "s1b" + name)

        start("s2z0", "s2z1")

    def fold_own():
        recv("O0")
        for a in (0, 1):
            add_rows(O.at[0, 0, a], [SB.at[0, a]])

    def fold_far(a):
        recv("O3%d" % a)
        add_rows(O.at[3, 0, a], [SB.at[3, a]])
        start("y0%d" % a, "y1%d" % a)

    def fold_half(h):
        piece = pl.ds(h * HT, HT)
        for i in (1, 2):
            recv("O%d%d" % (i, h))
            for a in (0, 1):
                add_rows(O.at[i, 0, a, piece], [SB.at[i, a, piece]])
        start("y%d3" % h, "y%d2" % h)

    def step(i, carry):
        @pl.when(i == 0)
        def _():
            recv("Xs0", "Cs0", "Gs0")

        @pl.when(i == 1)
        def _():
            partial(0, 1, True)
            recv("Gp", "Gm")
            start("Gs1", "Gs2", "Gf")
            recv("Xp0", "Cp0")
            start("Xf0", "Cf0")
            recv("Xm0", "Cm0")
            start("Xs1", "Cs1")
            recv("Gs1", "Gs2", "Xs1", "Cs1")

        @pl.when(i == 2)
        def _():
            partial(1, 1, False)
            recv("Gf")
            start("Gs3")
            recv("Xm1", "Cm1")
            start("Xf1", "Cf1")
            recv("Xp1", "Cp1")
            start("Xs2", "Cs2")
            fold_half(0)
            recv("Xs2", "Cs2")

        @pl.when(i == 3)
        def _():
            recv("Xf0")
            start("Xs30")
            recv("Xf1")
            start("Xs31")
            partial(2, 1, False)
            recv("Gs3", "Xs30", "Xs31")

        from_tokens(i)

        @pl.when(i == 3)
        def _():
            start("O30")
            recv("Cf0")
            start("Cs30")
            recv("Cf1")
            start("Cs31")
            fold_half(1)
            recv("Cs30", "Cs31")

        from_cotangents(i)

        @pl.when(i == 3)
        def _():
            finish()
            fold_far(0)

        token_grads(i)
        for k, names in ((0, ("O0",)), (1, ("O10", "O20")), (2, ("O11", "O21")), (3, ("O31",))):
            @pl.when(i == k)
            def _():
                start(*names)
        return carry

    lax.fori_loop(0, 4, step, 0)

    def y_final(p):
        recv("y%d2" % p, "y%d3" % p, "y%d4" % p, "y%d5" % p)

        @pl.loop(0, HT // 16)
        def _(i):
            sl = pl.ds(pl.multiple_of(p * HT + i * 16, 16), 16)
            mixed[sl, :] = (
                O[0, 0, 0, sl, :].astype(F32) + RY[3, sl, :].astype(F32) + RY[4, sl, :].astype(F32)
            ).astype(BF16)
            gtok[sl, :] = (
                O[0, 0, 1, sl, :].astype(F32) + RY[2, sl, :].astype(F32) + RY[5, sl, :].astype(F32)
            ).astype(BF16)

    def s3_turn():
        recv("s3zp1", "s3zm1")
        p_row = lax.broadcasted_iota(jnp.int32, (NX * 16, NX * per), 0)
        p_unit = lax.broadcasted_iota(jnp.int32, (NX * 16, NX * per), 1)
        apart = jnp.where(p_row == (p_unit // per) * 16 + p_unit % per, 1.0, 0.0).astype(BF16)

        @pl.loop(0, D // 1024)
        def _(n):
            cols = pl.ds(pl.multiple_of(n * 1024, 1024), 1024)
            total = S3[z, :, cols].astype(F32) + R3z[4, :, cols].astype(F32) + R3z[5, :, cols].astype(F32)
            S3x[:, :, cols] = dot(apart, total.astype(BF16)).astype(BF16).reshape(NX, 16, 1024)

        start("s3x0", "s3x1", "s3x2", "s3x3")

    def s2_turn():
        recv("s2zp1", "s2zm1")
        add_rows(f2(0), [R2z.at[4], R2z.at[5]])
        start("s2x0", "s2x1", "s2x2", "s2x3")

    def s3_end():
        recv("s3x2", "s3x3", "s3x4", "s3x5")
        low = a3(0)[...].astype(F32) + R3x[3].astype(F32) + R3x[4].astype(F32)
        high = b3(0)[...].astype(F32) + R3x[2].astype(F32) + R3x[5].astype(F32)
        for j in range(per):
            gdown[j, :, :hd] = low[j : j + 1]
            gdown[j, :, hd:] = high[j : j + 1]

    def s2_end():
        recv("s2x2", "s2x3", "s2x4", "s2x5")
        gup[:hr, CX - H :] = a2(0)[...].astype(F32) + R2x[3].astype(F32) + R2x[4].astype(F32)
        gup[hr:, CX - H :] = b2(0)[...].astype(F32) + R2x[2].astype(F32) + R2x[5].astype(F32)

    def s1_end(c):
        tag = ("s1a", "s1b")[c]
        recv(tag + "zp1", tag + "zm1")
        total = S1[c, x, z].astype(F32) + R1z[c, 4].astype(F32) + R1z[c, 5].astype(F32)
        if c == 0:
            ggate[:, : CX // 2] = total
        else:
            ggate[:, CX // 2 :] = total[:, : H - CX // 2]
            gup[:, : CX - H] = total[:, H - CX // 2 :]

    s3_hop(3)
    s2_hop(3)
    fold_far(1)
    fold_own()
    s1_mid[0]()
    s3_hop(2)
    s2_hop(2)
    s1_mid[1]()
    s1_turn(0)
    y_mid[0]()
    s3_hop(1)
    s1_turn(1)
    s2_hop(1)
    s1_hop[0](3)
    y_mid[1]()
    s3_turn()
    s1_hop[1](3)
    y_final(0)
    s2_turn()
    s1_hop[0](2)
    s3_mid()
    s1_hop[1](2)
    s2_mid()
    s1_hop[0](1)
    s3_end()
    s1_hop[1](1)
    y_final(1)
    s2_end()
    s1_end(0)
    s1_end(1)

    for n in copies:
        desc(n).wait_send()


def copy_kernel(*refs):
    half = len(refs) // 2
    for k in range(half):
        refs[half + k][...] = refs[k][...]


def per_device(tokens, expert_ids, gates, w_gate, w_up, w_down, cotangent):
    T, D = tokens.shape
    H = w_gate.shape[2]
    rows = D // (NX * NZ)
    per = H // (NX * NZ)
    hbm = pl.BlockSpec(memory_space=pl.ANY)
    vmem = pl.BlockSpec(memory_space=pltpu.VMEM)
    V = pltpu.VMEM
    CX = 512
    CZ = 2 * H - CX
    flops = 2 * 8 * T * D * H * 9
    shapes = (
        jax.ShapeDtypeStruct((T, D), BF16),
        jax.ShapeDtypeStruct((T, D), BF16),
        jax.ShapeDtypeStruct((rows, H), F32),
        jax.ShapeDtypeStruct((rows, H), F32),
        jax.ShapeDtypeStruct((per, 1, D), F32),
    )
    outs = pl.pallas_call(
        moe_kernel,
        out_shape=shapes,
        in_specs=[hbm, hbm, vmem, vmem, hbm, hbm, hbm],
        out_specs=(vmem,) * 5,
        scratch_shapes=[
            V((4, 2, 2, T // 2, D), BF16),
            V((4, 2, 2, T // 2, D), BF16),
            V((4, 2, 16, T), BF16),
            V((2, 2, T, 128), F32),
            V((8 * T, D), BF16),
            V((D, 2 * H), BF16),
            V((H, D), BF16),
            V((4, 2, 2, T, D), BF16),
            V((4, 2, T, D), BF16),
            V((6, T, D), BF16),
            V((8 * T, 2 * H), BF16),
            V((2 * T, H), BF16),
            V((2 * T, H), F32),
            V((2 * T, H), F32),
            V((2 * T, 128), F32),
            V((H, 8 * T), BF16),
            V((H, H), BF16),
            V((D, 2 * H), F32),
            V((H, D), F32),
            V((2, NX, NZ, rows, CX // 2), BF16),
            V((NZ, NX, rows, CZ), BF16),
            V((NZ, NX * per, D), BF16),
            V((NX, 16, D), BF16),
            V((2, 6, NZ // 2, rows, CX // 2), BF16),
            V((2, 2, rows // 2, CX // 2), BF16),
            V((2, 6, rows, CX // 2), BF16),
            V((2, NX // 2, rows, CZ), BF16),
            V((6, NX, rows, CZ), BF16),
            V((6, rows // 2, CZ), BF16),
            V((2, NX * per, D // 2), BF16),
            V((6, NX * per, D), BF16),
            V((6, 16, D // 2), BF16),
            pltpu.SemaphoreType.DMA((7,)),
            pltpu.SemaphoreType.DMA((COPIES,)),
            pltpu.SemaphoreType.DMA((COPIES,)),
        ],
        compiler_params=pltpu.CompilerParams(
            collective_id=0, has_side_effects=True, vmem_limit_bytes=63 * 2**20
        ),
        cost_estimate=pl.CostEstimate(flops=flops, bytes_accessed=32 << 20, transcendentals=8 * T * H),
        name="moe",
    )(tokens, cotangent, expert_ids.T, gates.T, w_gate[0], w_up[0], w_down[0])
    mixed, gtok, ggate, gup, gdown = pl.pallas_call(
        copy_kernel,
        out_shape=shapes,
        in_specs=[vmem] * 5,
        out_specs=(vmem,) * 5,
        name="hand_out",
    )(*outs)
    return mixed, gtok, ggate[None], gup[None], gdown.reshape(1, per, D)


def solution(mesh):
    return jax.shard_map(
        per_device,
        mesh=mesh,
        in_specs=(
            P(("dp", "expert"), None),
            P(("dp", "expert"), None),
            P(("dp", "expert"), None),
            P("expert", None, None),
            P("expert", None, None),
            P("expert", None, None),
            P(("dp", "expert"), None),
        ),
        out_specs=(
            P(("dp", "expert"), None),
            P(("dp", "expert"), None),
            P("expert", "dp", None),
            P("expert", "dp", None),
            P("expert", "dp", None),
        ),
        check_vma=False,
    )
```
